32 devices in a mesh: tm: 8 (over y, x, core), series: 4 (over z).
Axes of the slice: x: 2, y: 2, z: 4, core: 2. Of those that a mesh axis runs over, the one named last changes fastest.
Arguments:
- returns: bfloat16 [4096, 4096], P('tm', 'series'), may hold values from -120 to 120
- innovations: float32 [256, 2, 4096], P('series', None, 'tm'), may hold values from -6 to 6
- decay_rate: float32 [256, 4096], P('series', 'tm'), may hold values from 0.45 to 1
- innov_scale: float32 [256], P('series'), may hold values from 0.5 to 2
- loadings: bfloat16 [4096, 2, 256], P('series'), may hold values from -0.5 to 0.5
- noise_scale: float32 [4096], P('series'), may hold values from 0.5 to 2
Outputs:
- grad_innov: float32 [256, 2, 4096], P('series', None, 'tm')
- grad_load: float32 [4096, 2, 256], P('series')
- log_density: float32 [2], replicated
The draws below stay inside these ranges and needn't reach their ends.
All inputs are finite; a program needn't handle non-finite values.
Results may differ from the reference program's by a relative error of at most 0.00066.
Values may be sent and summed in bfloat16 or wider, within the bound.
No kernel may reach another device: no remote copies, remote signals or barrier semaphores. Data moves between devices by JAX's collectives and lax.ppermute only.
A program may use at most 64 MiB of HBM per device.

```python
import math
import jax
import jax.numpy as jnp
from jax import lax

HIDDEN_DRIVERS = 256
DRAWS = 2
T_DEV = 512
PERIOD_COUNT = 4096
SERIES = 4096


def draw_returns(key, part):
    key_base = jax.random.fold_in(jax.random.fold_in(key, 11), 0)
    time_pos = jnp.arange(PERIOD_COUNT, dtype=jnp.float32)[:, None] / PERIOD_COUNT
    series_pos = jnp.arange(SERIES, dtype=jnp.float32)[None, :] / SERIES
    base = jnp.clip(jax.random.normal(key_base, (PERIOD_COUNT, SERIES), jnp.float32), -6.0, 6.0)
    element_numbers = base * jnp.exp(1.4 * time_pos + 1.4 * series_pos)
    return jnp.clip(element_numbers, -120.0, 120.0).astype(jnp.bfloat16)


def draw_decay_rate(key, part):
    generator_seeds = jax.random.split(jax.random.fold_in(key, 23), 7)
    fast_rate = jnp.exp(jax.random.uniform(generator_seeds[0], (HIDDEN_DRIVERS, 1), jnp.float32, jnp.log(1.0 / 50.0), jnp.log(1.0 / 30.0)))
    slow_rate = jax.random.uniform(generator_seeds[1], (HIDDEN_DRIVERS, 1), jnp.float32, 0.3, 0.7) / PERIOD_COUNT
    fast_share = 0.5
    is_fast = jax.random.uniform(generator_seeds[2], (HIDDEN_DRIVERS, 1), jnp.float32) < fast_share
    base_rate = jnp.where(is_fast, fast_rate, slow_rate)
    block_factor = jnp.exp(jax.random.uniform(generator_seeds[3], (HIDDEN_DRIVERS, PERIOD_COUNT // T_DEV), jnp.float32, -0.69, 0.69))
    block_factor = jnp.repeat(block_factor, T_DEV, axis=1)
    jitter = jax.random.uniform(generator_seeds[4], (HIDDEN_DRIVERS, PERIOD_COUNT), jnp.float32, 0.7, 1.4)
    element_numbers = jnp.exp(-base_rate * block_factor * jitter)
    shock_location = jax.random.randint(generator_seeds[5], (HIDDEN_DRIVERS, 3), 0, PERIOD_COUNT)
    shock_scaling = jax.random.uniform(generator_seeds[6], (HIDDEN_DRIVERS, 3), jnp.float32, 0.5, 0.8)
    period_counter = jnp.arange(PERIOD_COUNT, dtype=jnp.int32)[None, :]
    shock_factor = jnp.ones((HIDDEN_DRIVERS, PERIOD_COUNT), jnp.float32)
    for shock_number in range(3):
        shock_flag_array = period_counter == shock_location[:, shock_number:shock_number + 1]
        shock_factor = jnp.minimum(shock_factor, jnp.where(shock_flag_array, shock_scaling[:, shock_number:shock_number + 1], 1.0))
    element_numbers = element_numbers * shock_factor
    return element_numbers.astype(jnp.float32)


def strengthened(drawn, rng, source, target, parts, factor):
    def block_of(position):
        return (jnp.arange(drawn.shape[position]) // (drawn.shape[position] // parts)).reshape((-1,) + (1,) * (drawn.ndim - 1 - position))

    near = jax.random.permutation(rng, parts)[block_of(target)]
    far = (block_of(target) + parts // 2) % parts
    return jnp.where((block_of(source) == near) | (block_of(source) == far), factor * drawn, drawn)


def level_of(rng, dims, pieces, low, top_value):
    def one(position, parts):
        steps = jax.random.uniform(jax.random.fold_in(jax.random.fold_in(rng, 6), position), (parts,), jnp.float32, low / len(pieces), top_value / len(pieces))
        return jnp.repeat(jnp.exp(steps), dims[position] // parts).reshape((-1,) + (1,) * (len(dims) - position - 1))

    loudness = one(*pieces[0])
    for cut in pieces[1:]:
        loudness = loudness * one(*cut)
    return loudness


def noise(key, dims, scale, reach, pieces=(), kind=jnp.bfloat16):
    array = jax.random.normal(key, dims, jnp.float32) * scale
    if len(pieces) > 0:
        array = level_of(key, dims, pieces, -0.22, 0.18) * array
    return jnp.clip(array, min=-reach, max=reach).astype(kind)


def bell_draw_with(stream_key, extent, width, limit, shards, heavy, kind=jnp.bfloat16):
    drawn = width * jax.random.normal(stream_key, extent, jnp.float32)
    if shards:
        drawn = drawn * level_of(stream_key, extent, shards, -0.22, 0.18)
    return jnp.clip(strengthened(drawn, jax.random.fold_in(stream_key, 3), *heavy), -limit, limit).astype(kind)


def setup_inputs(seed: int = 0) -> dict:
    key_list = jax.random.split(jax.random.key(seed), 7)
    return {
        "returns": draw_returns(jax.random.fold_in(key_list[6], 71), 0),
        "innovations": noise(key_list[1], (HIDDEN_DRIVERS, DRAWS, PERIOD_COUNT), 1.0, 6.0, ((0, 4), (2, 8)), jnp.float32),
        "decay_rate": draw_decay_rate(jax.random.fold_in(key_list[6], 71), 0),
        "innov_scale": jnp.clip(jnp.exp(math.log(2.0) - 1.3862944 * jax.random.uniform(key_list[3], (HIDDEN_DRIVERS,), jnp.float32) ** level_of(key_list[3], (HIDDEN_DRIVERS,), ((0, 4),), -0.2, 0.2)), 0.5, 2.0),
        "loadings": bell_draw_with(key_list[4], (SERIES, DRAWS, HIDDEN_DRIVERS), HIDDEN_DRIVERS ** -0.5, 0.5, ((0, 4),), (0, 2, 4, 2.0)),
        "noise_scale": jnp.clip(jnp.exp(math.log(2.0) - 1.3862944 * jax.random.uniform(key_list[5], (SERIES,), jnp.float32) ** level_of(key_list[5], (SERIES,), ((0, 4),), -0.2, 0.2)), 0.5, 2.0),
    }


freedom = 5.0

def affine_join(earlier, following):
    return (earlier[0] * following[0], following[0] * earlier[1] + following[1])

def reference(returns, innovations, decay_rate, innov_scale, loadings, noise_scale):
    factor_count, draw_count, time_count = innovations.shape
    series_count = returns.shape[1]
    spread = jnp.sqrt((1.0 - decay_rate) * (1.0 + decay_rate))
    weight_in = spread * innov_scale[:, None]
    pushes = weight_in[:, None, :] * innovations
    decays = jnp.broadcast_to(decay_rate[:, None, :], pushes.shape)
    _, factor_paths = lax.associative_scan(affine_join, (decays, pushes), axis=2)
    path_low = factor_paths.astype(jnp.bfloat16)
    load_wide = loadings.astype(jnp.float32)
    scale_sq = freedom * (noise_scale * noise_scale)
    block_len = math.gcd(time_count, 512)
    block_count = time_count // block_len

    def one_block(carried, block_idx):
        grad_acc, density_acc = carried
        row_start = (block_idx * block_len).astype(jnp.int32)
        rows_now = lax.dynamic_slice_in_dim(returns, row_start, block_len, 0).astype(jnp.float32)
        path_now = lax.dynamic_slice_in_dim(path_low, row_start, block_len, 2).astype(jnp.float32)
        fitted = jnp.einsum('kdt,sdk->dts', path_now, load_wide)
        residual = rows_now[None] - fitted
        density_acc = density_acc + lax.optimization_barrier(jnp.sum(-(freedom + 1.0) * 0.5 * jnp.log1p(residual * residual / scale_sq), axis=(1, 2)))
        pull_low = ((freedom + 1.0) * residual / (scale_sq + residual * residual)).astype(jnp.bfloat16)
        pull_low = lax.optimization_barrier(pull_low)
        pull_wide = pull_low.astype(jnp.float32)
        path_grad = jnp.einsum('dts,sdk->kdt', pull_wide, load_wide)
        grad_acc = grad_acc + jnp.einsum('dts,kdt->sdk', pull_wide, path_now)
        return ((grad_acc, density_acc), path_grad)
    start_state = (jnp.zeros(loadings.shape, jnp.float32), jnp.zeros((draw_count,), jnp.float32))
    (grad_load, density_sum), grad_blocks = lax.scan(one_block, start_state, jnp.arange(block_count, dtype=jnp.int32))
    path_grads = jnp.transpose(grad_blocks, (1, 2, 0, 3)).reshape(factor_count, draw_count, time_count)
    shifted = jnp.concatenate([decay_rate[:, 1:], jnp.ones((factor_count, 1), jnp.float32)], axis=1)
    shifts = jnp.broadcast_to(shifted[:, None, :], path_grads.shape)
    _, adjoint = lax.associative_scan(affine_join, (shifts, path_grads), reverse=True, axis=2)
    grad_innov = weight_in[:, None, :] * adjoint - innovations
    log_density = (density_sum - 0.5 * lax.optimization_barrier(jnp.sum(innovations * innovations, axis=(0, 2)))) / (time_count * series_count)
    return (grad_innov, grad_load, log_density)
```

```python
import functools

import jax
import jax.numpy as jnp
from jax import lax
from jax.experimental import pallas as pl
from jax.experimental.pallas import tpu as pltpu
from jax.sharding import PartitionSpec as P


freedom = 5.0
LANES = 128
f32 = jnp.float32
bf16 = jnp.bfloat16
f16 = jnp.float16


def swap(value, axis, key):
    count = lax.axis_size(axis)
    return lax.ppermute(value, axis, [(i, i ^ key) for i in range(count)])


def eye(size):
    rows = lax.broadcasted_iota(jnp.int32, (size, size), 0)
    return rows == lax.broadcasted_iota(jnp.int32, (size, size), 1)


def to_column(row, same):
    return jnp.sum(jnp.where(same, row, 0.0), axis=1, keepdims=True)


def to_row(column, same):
    return jnp.sum(jnp.where(same, column, 0.0), axis=0, keepdims=True)


def tile_scan(decay, pushes, backward):
    lane = lax.broadcasted_iota(jnp.int32, decay.shape, 1)
    width = decay.shape[1]
    step = 1
    while step < width:
        turn = width - step if backward else step
        inside = lane < width - step if backward else lane >= step
        gate = jnp.where(inside, decay, 0.0)
        pushes = [p + gate * pltpu.roll(p, turn, 1) for p in pushes]
        decay = decay * jnp.where(inside, pltpu.roll(decay, turn, 1), 1.0)
        step *= 2
    return decay, pushes


def block_scan(decays, pushes, backward):
    tiles = len(decays)
    draws = len(pushes[0])
    order = range(tiles - 1, -1, -1) if backward else range(tiles)
    edge = slice(0, 1) if backward else slice(LANES - 1, LANES)
    run, out = [None] * tiles, [None] * tiles
    carry = None
    for j in order:
        a, b = tile_scan(decays[j], pushes[j], backward)
        if carry is not None:
            b = [b[d] + a * carry[1][d] for d in range(draws)]
            a = a * carry[0]
        run[j], out[j] = a, b
        carry = (a[:, edge], [x[:, edge] for x in b])
    return run, out, carry


def forward_kernel(draws, tiles, innov, decay, scale, local, running, weight, summary, squares):
    factors = decay.shape[0]
    same = eye(factors)
    column = to_column(scale[...], same)
    decays, pushes = [], []
    total = [jnp.zeros((factors, LANES), f32)] * draws
    for j in range(tiles):
        a = decay[:, j * LANES:(j + 1) * LANES]
        w = jnp.sqrt((1.0 - a) * (1.0 + a)) * column
        weight[:, j * LANES:(j + 1) * LANES] = w
        x = [innov[pl.ds(j * draws + d, factors, stride=tiles * draws), :] for d in range(draws)]
        total = [total[d] + x[d] * x[d] for d in range(draws)]
        decays.append(a)
        pushes.append([w * x[d] for d in range(draws)])
    run, out, carry = block_scan(decays, pushes, False)
    for j in range(tiles):
        running[:, j * LANES:(j + 1) * LANES] = run[j]
        for d in range(draws):
            local[d, :, j * LANES:(j + 1) * LANES] = out[j][d]
    summary[0:1, :] = to_row(carry[0], same)
    for d in range(draws):
        summary[d + 1:d + 2, :] = to_row(carry[1][d], same)
        squares[d:d + 1, :] = jnp.sum(total[d], axis=0, keepdims=True)


def enter_kernel(draws, local, running, entering, path):
    same = eye(running.shape[0])
    for d in range(draws):
        column = to_column(entering[d:d + 1, :], same)
        path[d] = (local[d] + running[...] * column).astype(bf16)


def residual_kernel(draws, parts, order, *refs):
    pieces, (returns, loads, loads_t, scale, pull, grads, paths, density) = refs[:parts], refs[parts:]
    factors = pieces[0].shape[1]
    step = pl.program_id(0)

    @pl.when(step == 0)
    def _():
        for n in range(parts):
            start = pl.multiple_of(order[n] * factors, factors)
            paths[:, pl.ds(start, factors), :] = pieces[n][...]
        grads[...] = jnp.zeros_like(grads)
        density[...] = jnp.zeros_like(density)

    seen = returns[...].astype(f32)
    s2 = scale[...]
    inverse = 1.0 / s2
    rows = seen.shape[0]
    half = rows // 2
    for d in range(draws):
        fitted = jnp.dot(loads[d], paths[d], preferred_element_type=f32)
        residual = seen - fitted
        square = residual * residual
        pulled = ((freedom + 1.0) * residual / (s2 + square)).astype(bf16)
        pull[d] = pulled
        ratio = square * inverse
        first, second = ratio[:half], ratio[half:]
        both = jnp.log1p(first + second * (1.0 + first))
        both = jnp.sum(both, axis=0, keepdims=True)
        lanes = both[:, :LANES]
        for j in range(1, both.shape[1] // LANES):
            lanes = lanes + both[:, j * LANES:(j + 1) * LANES]
        density[d:d + 1, :] += lanes
        product = jnp.dot(loads_t[d], pulled, preferred_element_type=f32)
        for n in range(parts):
            grads[n, d] += product[n * factors:(n + 1) * factors, :]


def load_kernel(draws, pull, paths, out):
    rows = pull.shape[1]
    tiles = paths.shape[1] // LANES
    for d in range(draws):
        share = lax.dot_general(pull[d], paths[d], (((1,), (1,)), ((), ())), preferred_element_type=f32)
        for j in range(tiles):
            out[pl.ds(j * draws + d, rows, stride=tiles * draws), :] = share[:, j * LANES:(j + 1) * LANES]


def backward_kernel(draws, tiles, decay, grads, local, tail, summary):
    factors = decay.shape[0]
    same = eye(factors)
    lane = lax.broadcasted_iota(jnp.int32, (factors, LANES), 1)
    decays, pushes = [], []
    for j in range(tiles):
        a = decay[:, j * LANES:(j + 1) * LANES]
        if j + 1 < tiles:
            after = decay[:, (j + 1) * LANES:(j + 2) * LANES][:, 0:1]
        else:
            after = jnp.ones((factors, 1), f32)
        decays.append(jnp.where(lane < LANES - 1, pltpu.roll(a, LANES - 1, 1), after))
        pushes.append([grads[d, :, j * LANES:(j + 1) * LANES] for d in range(draws)])
    run, out, carry = block_scan(decays, pushes, True)
    for j in range(tiles):
        tail[:, j * LANES:(j + 1) * LANES] = run[j]
        for d in range(draws):
            local[d, :, j * LANES:(j + 1) * LANES] = out[j][d]
    first = decay[:, 0:LANES][:, 0:1]
    summary[0:1, :] = to_row(first * carry[0], same)
    for d in range(draws):
        summary[d + 1:d + 2, :] = to_row(first * carry[1][d], same)


def leave_kernel(draws, tiles, local, tail, weight, innov, arriving, out):
    factors = tail.shape[0]
    same = eye(factors)
    for d in range(draws):
        column = to_column(arriving[d:d + 1, :], same)
        for j in range(tiles):
            part = slice(j * LANES, (j + 1) * LANES)
            rows = pl.ds(j * draws + d, factors, stride=tiles * draws)
            adjoint = local[d, :, part] + tail[:, part] * column
            out[rows, :] = weight[:, part] * adjoint - innov[rows, :]


def shape(dims, kind):
    return jax.ShapeDtypeStruct(dims, kind)


def carried(summary, extra, axis, backward):
    count, mine = lax.axis_size(axis), lax.axis_index(axis)
    rows = summary.shape[0]
    if extra is not None:
        summary = jnp.concatenate([summary, extra], axis=0)
    if backward:
        mine = count - 1 - mine
    other = swap(summary, axis, 1)
    later = mine % 2 == 1
    first, second = jnp.where(later, other, summary), jnp.where(later, summary, other)
    joined = [first[:1] * second[:1], second[:1] * first[1:rows] + second[1:rows]]
    if extra is not None:
        joined.append(first[rows:] + second[rows:])
    whole = jnp.concatenate(joined, axis=0)
    pairs, pair = count // 2, mine // 2
    totals = [whole] + [swap(whole, axis, 2 * key) for key in range(1, pairs)]
    entering = jnp.zeros_like(summary[1:rows])
    summed = jnp.zeros_like(summary[rows:])
    for place in range(pairs):
        here = totals[0]
        for key in range(1, pairs):
            here = jnp.where((pair ^ key) == place, totals[key], here)
        entering = jnp.where(place < pair, here[:1] * entering + here[1:rows], entering)
        summed = summed + here[rows:]
    return jnp.where(later, other[:1] * entering + other[1:rows], entering), summed


def local(returns, innovations, decay_rate, innov_scale, loadings, noise_scale):
    factors, draws, steps = innovations.shape
    series = returns.shape[1]
    parts, spans = lax.axis_size("series"), lax.axis_size("tm")
    where, when = lax.axis_index("series"), lax.axis_index("tm")
    tiles = steps // LANES
    all_factors = factors * parts

    innov = innovations.reshape(factors, draws, tiles, LANES).transpose(0, 2, 1, 3)
    innov = innov.reshape(factors * tiles * draws, LANES)
    local_paths, running, weight, summary, squares = pl.pallas_call(
        functools.partial(forward_kernel, draws, tiles),
        out_shape=(
            shape((draws, factors, steps), f32),
            shape((factors, steps), f32),
            shape((factors, steps), f32),
            shape((draws + 1, factors), f32),
            shape((draws, LANES), f32),
        ),
        name="forward_scan",
    )(innov, decay_rate, innov_scale.reshape(1, factors))
    entering, _ = carried(summary, None, "tm", False)
    path_low = pl.pallas_call(
        functools.partial(enter_kernel, draws),
        out_shape=shape((draws, factors, steps), bf16),
        name="enter",
    )(local_paths, running, entering)

    pieces = [path_low] + [swap(path_low, "series", key) for key in range(1, parts)]
    order = jnp.bitwise_xor(where, jnp.arange(parts, dtype=jnp.int32)).astype(jnp.int32)
    scale_sq = (freedom * (noise_scale * noise_scale)).reshape(series, 1)
    seen = returns.T
    loads = loadings.transpose(1, 0, 2)
    loads_t = loadings.transpose(1, 2, 0)
    rows = min(256, series)
    still = lambda dims: pl.BlockSpec(dims, lambda i, o: (0,) * len(dims))
    pull, grads, paths, density = pl.pallas_call(
        functools.partial(residual_kernel, draws, parts),
        out_shape=(
            shape((draws, series, steps), bf16),
            shape((parts, draws, factors, steps), f32),
            shape((draws, all_factors, steps), bf16),
            shape((draws, LANES), f32),
        ),
        grid_spec=pltpu.PrefetchScalarGridSpec(
            num_scalar_prefetch=1,
            grid=(series // rows,),
            in_specs=[still((draws, factors, steps))] * parts
            + [
                pl.BlockSpec((rows, steps), lambda i, o: (i, 0)),
                pl.BlockSpec((draws, rows, all_factors), lambda i, o: (0, i, 0)),
                pl.BlockSpec((draws, all_factors, rows), lambda i, o: (0, 0, i)),
                pl.BlockSpec((rows, 1), lambda i, o: (i, 0)),
            ],
            out_specs=[
                pl.BlockSpec((draws, rows, steps), lambda i, o: (0, i, 0)),
                still((parts, draws, factors, steps)),
                still((draws, all_factors, steps)),
                still((draws, LANES)),
            ],
        ),
        name="residual",
    )(order, *pieces, seen, loads, loads_t, scale_sq)

    def share_of(place):
        return lax.dynamic_index_in_dim(grads, place, 0, keepdims=False)

    path_up = 32.0
    path_grads = share_of(where)
    for key in range(1, parts):
        sent = (share_of(where ^ key) * path_up).astype(f16)
        path_grads = path_grads + swap(sent, "series", key).astype(f32) * (1.0 / path_up)

    wide = all_factors * draws // LANES
    load_share = pl.pallas_call(
        functools.partial(load_kernel, draws),
        out_shape=shape((series * wide, LANES), f32),
        grid=(series // rows,),
        in_specs=[
            pl.BlockSpec((draws, rows, steps), lambda i: (0, i, 0)),
            pl.BlockSpec((draws, all_factors, steps), lambda i: (0, 0, 0)),
        ],
        out_specs=pl.BlockSpec((rows * wide, LANES), lambda i: (i, 0)),
        name="load_grads",
    )(pull, paths)

    down = 1.0 / 1024.0
    size = series * wide
    core, chip, chips = when % 2, when // 2, spans // 2
    half, piece = size // 2, size // spans
    kept = lax.dynamic_slice_in_dim(load_share, core * half, half, 0)
    sent = (lax.dynamic_slice_in_dim(load_share, (1 - core) * half, half, 0) * down).astype(f16)
    kept = kept + swap(sent, "tm", 1).astype(f32) * (1.0 / down)
    total = lax.dynamic_slice_in_dim(kept, chip * piece, piece, 0)
    for key in range(1, chips):
        sent = (lax.dynamic_slice_in_dim(kept, (chip ^ key) * piece, piece, 0) * down).astype(f16)
        total = total + swap(sent, "tm", 2 * key).astype(f32) * (1.0 / down)
    total = (total * down).astype(f16)
    mine = jnp.zeros((half, LANES), f16)
    mine = lax.dynamic_update_slice_in_dim(mine, total, chip * piece, 0)
    for key in range(1, chips):
        mine = lax.dynamic_update_slice_in_dim(mine, swap(total, "tm", 2 * key), (chip ^ key) * piece, 0)
    theirs = swap(mine, "tm", 1)
    low, high = jnp.where(core == 0, mine, theirs), jnp.where(core == 0, theirs, mine)
    grad_load = jnp.concatenate([low, high], axis=0).astype(f32) * (1.0 / down)
    grad_load = grad_load.reshape(series, all_factors // LANES, draws, LANES).transpose(0, 2, 1, 3)
    grad_load = grad_load.reshape(series, draws, all_factors)

    partial = jnp.sum(-(freedom + 1.0) * 0.5 * density - 0.5 * squares, axis=1, keepdims=True)
    key = 1
    while key < parts:
        partial = partial + swap(partial, "series", key)
        key *= 2
    local_adjoint, tail, summary = pl.pallas_call(
        functools.partial(backward_kernel, draws, tiles),
        out_shape=(
            shape((draws, factors, steps), f32),
            shape((factors, steps), f32),
            shape((draws + 1, factors), f32),
        ),
        name="backward_scan",
    )(decay_rate, path_grads)
    arriving, density = carried(summary, jnp.broadcast_to(partial, (draws, factors)), "tm", True)
    grad_innov = pl.pallas_call(
        functools.partial(leave_kernel, draws, tiles),
        out_shape=shape(innov.shape, f32),
        name="leave",
    )(local_adjoint, tail, weight, innov, arriving)
    grad_innov = grad_innov.reshape(factors, tiles, draws, LANES).transpose(0, 2, 1, 3)
    grad_innov = grad_innov.reshape(factors, draws, steps)

    log_density = density[:, 0] / (steps * spans * series * parts)
    return (grad_innov, grad_load, log_density)


def solution(mesh):
    placed = (
        P("tm", "series"),
        P("series", None, "tm"),
        P("series", "tm"),
        P("series"),
        P("series", None, None),
        P("series"),
    )
    return jax.shard_map(
        local,
        mesh=mesh,
        in_specs=placed,
        out_specs=(P("series", None, "tm"), P("series", None, None), P()),
        check_vma=False,
    )
```

```python
import functools
import math

import jax
import jax.numpy as jnp
from jax import lax
from jax.experimental import pallas as pl
from jax.experimental.pallas import tpu as pltpu
from jax.sharding import PartitionSpec as P


freedom = 5.0
LANES = 128
TAIL = 16
f32 = jnp.float32
bf16 = jnp.bfloat16
f16 = jnp.float16


def swap(value, axis, key):
    count = lax.axis_size(axis)
    return lax.ppermute(value, axis, [(i, i ^ key) for i in range(count)])


def eye(size):
    rows = lax.broadcasted_iota(jnp.int32, (size, size), 0)
    return rows == lax.broadcasted_iota(jnp.int32, (size, size), 1)


def to_column(row, same):
    return jnp.sum(jnp.where(same, row, 0.0), axis=1, keepdims=True)


def to_row(column, same):
    return jnp.sum(jnp.where(same, column, 0.0), axis=0, keepdims=True)


def tile_scan(decay, pushes, backward):
    lane = lax.broadcasted_iota(jnp.int32, decay.shape, 1)
    width = decay.shape[1]
    step = 1
    while step < width:
        turn = width - step if backward else step
        inside = lane < width - step if backward else lane >= step
        gate = jnp.where(inside, decay, 0.0)
        pushes = [p + gate * pltpu.roll(p, turn, 1) for p in pushes]
        decay = decay * jnp.where(inside, pltpu.roll(decay, turn, 1), 1.0)
        step *= 2
    return decay, pushes


def block_scan(decays, pushes, backward):
    tiles = len(decays)
    draws = len(pushes[0])
    order = range(tiles - 1, -1, -1) if backward else range(tiles)
    edge = slice(0, 1) if backward else slice(LANES - 1, LANES)
    run, out = [None] * tiles, [None] * tiles
    carry = None
    for j in order:
        a, b = tile_scan(decays[j], pushes[j], backward)
        if carry is not None:
            b = [b[d] + a * carry[1][d] for d in range(draws)]
            a = a * carry[0]
        run[j], out[j] = a, b
        carry = (a[:, edge], [x[:, edge] for x in b])
    return run, out, carry


def beyond_kernel(tiles, decay, spread, beyond, product):
    factors = decay.shape[0]
    lane = lax.broadcasted_iota(jnp.int32, (factors, LANES), 1)
    after = jnp.ones((factors, 1), f32)
    for j in range(tiles - 1, -1, -1):
        part = slice(j * LANES, (j + 1) * LANES)
        a = decay[:, part]
        spread[:, part] = jnp.sqrt((1.0 - a) * (1.0 + a))
        run, _ = tile_scan(a, [], True)
        beyond[:, part] = jnp.where(lane < LANES - 1, pltpu.roll(run, LANES - 1, 1), 1.0) * after
        after = after * run[:, 0:1]
    product[...] = to_row(after, eye(factors))


def edge_kernel(draws, tiles, innov, scale, spread, beyond, product, weight, summary, squares):
    factors = spread.shape[0]
    same = eye(factors)
    column = to_column(scale[...], same)
    total = [jnp.zeros((factors, LANES), f32)] * draws
    ends = [jnp.zeros((factors, LANES), f32)] * draws
    for j in range(tiles):
        part = slice(j * LANES, (j + 1) * LANES)
        w = spread[:, part] * column
        weight[:, part] = w
        for d in range(draws):
            x = innov[pl.ds(j * draws + d, factors, stride=tiles * draws), :]
            total[d] = total[d] + x * x
            ends[d] = ends[d] + w * x * beyond[:, part]
    summary[0:1, :] = product[...]
    for d in range(draws):
        summary[d + 1:d + 2, :] = to_row(jnp.sum(ends[d], axis=1, keepdims=True), same)
        squares[d:d + 1, :] = jnp.sum(total[d], axis=0, keepdims=True)


def forward_kernel(draws, tiles, innov, decay, weight, local, running):
    factors = decay.shape[0]
    decays, pushes = [], []
    for j in range(tiles):
        part = slice(j * LANES, (j + 1) * LANES)
        decays.append(decay[:, part])
        rows = lambda d: pl.ds(j * draws + d, factors, stride=tiles * draws)
        pushes.append([weight[:, part] * innov[rows(d), :] for d in range(draws)])
    run, out, _ = block_scan(decays, pushes, False)
    for j in range(tiles):
        running[:, j * LANES:(j + 1) * LANES] = run[j]
        for d in range(draws):
            local[d, :, j * LANES:(j + 1) * LANES] = out[j][d]


def seat(backward):
    count, mine = lax.axis_size("tm"), lax.axis_index("tm")
    return count - 1 - mine if backward else mine


def pair_kernel(rows, backward, summary, other, whole):
    later = seat(backward) % 2 == 1
    mine, theirs = summary[...], other[...]
    first, second = jnp.where(later, theirs, mine), jnp.where(later, mine, theirs)
    whole[0:1, :] = first[0:1] * second[0:1]
    whole[1:rows, :] = second[0:1] * first[1:rows] + second[1:rows]
    if rows < mine.shape[0]:
        whole[rows:, :] = first[rows:] + second[rows:]


def entered(rows, backward, other, totals):
    mine = seat(backward)
    later, pair, pairs = mine % 2 == 1, mine // 2, len(totals)
    theirs = other[...]
    values = [total[...] for total in totals]
    entering = jnp.zeros_like(theirs[1:rows])
    summed = jnp.zeros_like(theirs[rows:]) if rows < theirs.shape[0] else None
    for place in range(pairs):
        here = values[0]
        for key in range(1, pairs):
            here = jnp.where((pair ^ key) == place, values[key], here)
        entering = jnp.where(place < pair, here[0:1] * entering + here[1:rows], entering)
        if summed is not None:
            summed = summed + here[rows:]
    return jnp.where(later, theirs[0:1] * entering + theirs[1:rows], entering), summed


def enter_kernel(draws, local, running, other, *refs):
    totals, path = refs[:-1], refs[-1]
    same = eye(running.shape[0])
    entering, _ = entered(draws + 1, False, other, totals)
    for d in range(draws):
        column = to_column(entering[d:d + 1, :], same)
        path[d] = (local[d] + running[...] * column).astype(bf16)


def residual_kernel(draws, parts, *refs):
    pieces, (returns, loads, loads_t, noise, squares, grads, shares, paths, density, top) = refs[:parts], refs[parts:]
    factors = pieces[0].shape[1]
    step = pl.program_id(0)
    count = pl.num_programs(0)
    wide = paths.shape[1] // LANES
    side = step // (count // 2)
    base = (step % (count // 2)) * (returns.shape[0] * wide * draws)

    @pl.when(step == 0)
    def _():
        for n in range(parts):
            start = pl.multiple_of((lax.axis_index("series") ^ n) * factors, factors)
            paths[:, pl.ds(start, factors), :] = pieces[n][...]
        grads[...] = jnp.zeros_like(grads)
        density[...] = jnp.zeros_like(density)
        top[...] = jnp.zeros_like(top)

    seen = returns[...].astype(f32)
    rows = seen.shape[0]
    same = eye(LANES)
    groups = rows // LANES
    spread = [to_column(noise[pl.ds(step * groups + g, 1), :], same) for g in range(groups)]
    spread = jnp.concatenate(spread, axis=0)
    s2 = freedom * (spread * spread)
    inverse = 1.0 / s2
    tiles = seen.shape[1] // LANES
    half = rows // 2
    for d in range(draws):
        fitted = jnp.dot(loads[d], paths[d], preferred_element_type=f32)
        residual = seen - fitted
        square = residual * residual
        pulled = ((freedom + 1.0) * residual / (s2 + square)).astype(bf16)
        ratio = square * inverse
        first, second = ratio[:half], ratio[half:]
        both = jnp.log1p(first + second * (1.0 + first))
        both = jnp.sum(both, axis=0, keepdims=True)
        lanes = both[:, :LANES]
        for j in range(1, both.shape[1] // LANES):
            lanes = lanes + both[:, j * LANES:(j + 1) * LANES]
        density[d:d + 1, :] += lanes
        product = jnp.dot(loads_t[d], pulled, preferred_element_type=f32)
        for n in range(parts):
            for j in range(tiles):
                to = slice((d * tiles + j) * factors, (d * tiles + j + 1) * factors)
                grads[n, to, :] += product[n * factors:(n + 1) * factors, j * LANES:(j + 1) * LANES]
        share = lax.dot_general(pulled, paths[d], (((1,), (1,)), ((), ())), preferred_element_type=f32)
        most = top[...]
        for j in range(wide):
            tile = share[:, j * LANES:(j + 1) * LANES]
            shares[side, pl.ds(base + (j * draws + d), rows, stride=wide * draws), :] = tile
            most = jnp.maximum(most, jnp.max(jnp.abs(tile).reshape(rows // 8, 8, LANES), axis=0))
        top[...] = most

    @pl.when(step == pl.num_programs(0) - 1)
    def _():
        body = draws * tiles * factors
        cells = pl.num_programs(0) * rows * seen.shape[1]
        peak = jnp.zeros((1, LANES), f32)
        for n in range(parts):
            peak = jnp.maximum(peak, jnp.max(jnp.abs(grads[n, :body, :]), axis=0, keepdims=True))
        level = exponent(peak)
        tail = [level]
        for d in range(draws):
            value = -(freedom + 1.0) * 0.5 * density[d:d + 1, :] - 0.5 * squares[d:d + 1, :]
            tail += coded(jnp.sum(value, axis=1, keepdims=True) * (1.0 / cells))
        tail = stacked(tail)
        factor = jnp.exp2(15.0 - level)
        for n in range(parts):
            grads[n, :body, :] = grads[n, :body, :] * factor
            grads[n, body:, :] = tail
        half = shares.shape[1] - TAIL
        level = exponent(jnp.max(top[...], axis=0, keepdims=True))
        factor = jnp.exp2(15.0 - level)
        for n in range(2):
            shares[n, :half, :] = shares[n, :half, :] * factor
            shares[n, half:, :] = stacked([level])


def coded(value):
    value = jnp.broadcast_to(value, (1, LANES))
    level = exponent(jnp.abs(value))
    left = value * jnp.exp2(-level)
    codes = [level]
    unit = 1024.0
    for _ in range(3):
        code = (left * unit + 12582912.0) - 12582912.0
        codes.append(code)
        left = left - code * (1.0 / unit)
        unit = unit * 1024.0
    return codes


def decoded(rows):
    level, first, second, third = [rows[n:n + 1, :] for n in range(4)]
    small = 1.0 / 1024.0
    return jnp.exp2(level) * (first + (second + third * small) * small) * small


def stacked(rows):
    place = lax.broadcasted_iota(jnp.int32, (TAIL, LANES), 0)
    out = jnp.zeros((TAIL, LANES), f32)
    for n, row in enumerate(rows):
        out = jnp.where(place == n, row, out)
    return out


def exponent(lanes):
    top = jnp.maximum(jnp.max(lanes, axis=1, keepdims=True), 1e-30)
    return jnp.broadcast_to(jnp.ceil(jnp.log(top) * (1.0 / math.log(2.0))), lanes.shape)


def join_kernel(mine, other, out):
    core = lax.axis_index("tm") % 2
    body = other.shape[0] - TAIL
    chips = out.shape[0]
    piece = body // chips
    own, far = mine[core, body:body + 1, :], other[body:body + 1, :]
    level = jnp.maximum(own, far) + 1.0
    own, far = jnp.exp2(own - level), jnp.exp2(far - level)
    for n in range(chips):
        rows = slice(n * piece, (n + 1) * piece)
        out[n, :piece, :] = mine[core, rows, :] * own + other[rows, :] * far
        out[n, piece:, :] = stacked([level])


def total_kernel(lift, mine, *refs):
    others, (out, factor) = refs[:-2], refs[-2:]
    piece = out.shape[0]
    here = lax.axis_index("tm") // 2
    levels = [mine[here, piece:piece + 1, :]] + [other[piece:piece + 1, :] for other in others]
    top = levels[0]
    for level in levels[1:]:
        top = jnp.maximum(top, level)
    top = top + lift
    total = mine[here, :piece, :] * jnp.exp2(levels[0] - top)
    for level, other in zip(levels[1:], others):
        total = total + other[:piece, :] * jnp.exp2(level - top)
    out[...] = total
    factor[...] = jnp.exp2(top - 15.0)


def gather_kernel(draws, tiles, parts, running, products, mine, *refs):
    others, (gathered, summary) = refs[:-2], refs[-2:]
    factors = running.shape[0]
    body = draws * tiles * factors
    here = lax.axis_index("series")
    tails = [mine[here, body:, :]] + [other[body:, :] for other in others]
    scales = [jnp.exp2(rows[0:1, :] - 15.0) for rows in tails]
    same = eye(factors)
    summary[0:1, :] = products[0:1, :]
    for d in range(draws):
        known = [decoded(rows[1 + 4 * d:5 + 4 * d, :]) for rows in tails]
        density = jnp.zeros((1, LANES), f32)
        for place in range(parts):
            for n in range(parts):
                density = density + jnp.where((here ^ n) == place, known[n], 0.0)
        summary[draws + 1 + d:draws + 2 + d, :] = density[:, :factors]
        leaving = jnp.zeros((factors, LANES), f32)
        for j in range(tiles):
            rows = slice((d * tiles + j) * factors, (d * tiles + j + 1) * factors)
            value = mine[here, rows, :] * scales[0]
            for other, scale in zip(others, scales[1:]):
                value = value + other[rows, :] * scale
            gathered[rows, :] = value
            leaving = leaving + value * running[:, j * LANES:(j + 1) * LANES]
        summary[d + 1:d + 2, :] = to_row(jnp.sum(leaving, axis=1, keepdims=True), same)


def backward_kernel(draws, tiles, decay, grads, local, tail):
    factors = decay.shape[0]
    lane = lax.broadcasted_iota(jnp.int32, (factors, LANES), 1)
    decays, pushes = [], []
    for j in range(tiles):
        a = decay[:, j * LANES:(j + 1) * LANES]
        if j + 1 < tiles:
            after = decay[:, (j + 1) * LANES:(j + 2) * LANES][:, 0:1]
        else:
            after = jnp.ones((factors, 1), f32)
        decays.append(jnp.where(lane < LANES - 1, pltpu.roll(a, LANES - 1, 1), after))
        rows = lambda d: slice((d * tiles + j) * factors, (d * tiles + j + 1) * factors)
        pushes.append([grads[rows(d), :] for d in range(draws)])
    run, out, _ = block_scan(decays, pushes, True)
    for j in range(tiles):
        tail[:, j * LANES:(j + 1) * LANES] = run[j]
        for d in range(draws):
            local[d, :, j * LANES:(j + 1) * LANES] = out[j][d]


def leave_kernel(draws, tiles, local, tail, weight, innov, other, *refs):
    totals, (out, density) = refs[:-2], refs[-2:]
    factors = tail.shape[0]
    same = eye(factors)
    arriving, summed = entered(draws + 1, True, other, totals)
    density[...] = summed
    for d in range(draws):
        column = to_column(arriving[d:d + 1, :], same)
        for j in range(tiles):
            part = slice(j * LANES, (j + 1) * LANES)
            rows = pl.ds(j * draws + d, factors, stride=tiles * draws)
            adjoint = local[d, :, part] + tail[:, part] * column
            out[rows, :] = weight[:, part] * adjoint - innov[rows, :]


def room(mebibytes):
    return pltpu.CompilerParams(vmem_limit_bytes=mebibytes << 20)


def assemble_kernel(*refs):
    pieces, out = refs[:-1], refs[-1]
    rows = pieces[0].shape[0]
    for key, piece in enumerate(pieces):
        start = pl.multiple_of(((lax.axis_index("tm") // 2) ^ key) * rows, rows)
        out[pl.ds(start, rows), :] = piece[...]


def write_kernel(flip, value, factor, *refs):
    out, scaled, sem = refs[-3:]
    half = value.shape[0]
    scaled[...] = value[...] * factor[...]
    move = pltpu.make_async_copy(scaled, out.at[pl.ds(pl.multiple_of(((lax.axis_index("tm") + flip) % 2) * half, half), half), :], sem)
    move.start()
    move.wait()


def write_half(value, factor, flip, out, size):
    far = pl.BlockSpec(memory_space=pltpu.HBM)
    specs = [pl.BlockSpec(memory_space=pltpu.VMEM)] * 2
    return pl.pallas_call(
        functools.partial(write_kernel, flip),
        out_shape=shape((size, LANES), f32),
        in_specs=specs if out is None else specs + [far],
        out_specs=far,
        input_output_aliases={} if out is None else {2: 0},
        scratch_shapes=[pltpu.VMEM(value.shape, f32), pltpu.SemaphoreType.DMA],
        name="write_half",
        compiler_params=room(4),
    )(value, factor, *([] if out is None else [out]))


def shape(dims, kind):
    return jax.ShapeDtypeStruct(dims, kind)


def carried(summary, rows, backward):
    pairs = lax.axis_size("tm") // 2
    other = swap(summary, "tm", 1)
    whole = pl.pallas_call(
        functools.partial(pair_kernel, rows, backward),
        out_shape=shape(summary.shape, f32),
        compiler_params=room(1),
    )(summary, other)
    return [other, whole] + [swap(whole, "tm", 2 * key) for key in range(1, pairs)]


def local(returns, innovations, decay_rate, innov_scale, loadings, noise_scale):
    factors, draws, steps = innovations.shape
    series = returns.shape[1]
    parts, spans = lax.axis_size("series"), lax.axis_size("tm")
    where, when = lax.axis_index("series"), lax.axis_index("tm")
    tiles = steps // LANES
    all_factors = factors * parts
    wide = all_factors * draws // LANES

    innov = innovations.reshape(factors, draws, tiles, LANES).transpose(0, 2, 1, 3)
    innov = innov.reshape(factors * tiles * draws, LANES)
    numbers = [where ^ key for key in range(parts)] + [1 - when % 2]
    numbers += [(when // 2) ^ key for key in range(spans // 2)]
    decay_rate, numbers = lax.optimization_barrier((decay_rate, numbers))
    seats, far_core = numbers[:parts], numbers[parts]
    chips_at = numbers[parts + 1:]
    spread, beyond, product = pl.pallas_call(
        functools.partial(beyond_kernel, tiles),
        out_shape=(shape((factors, steps), f32), shape((factors, steps), f32), shape((1, factors), f32)),
        name="beyond",
        compiler_params=room(2),
    )(decay_rate)
    weight, summary, squares = pl.pallas_call(
        functools.partial(edge_kernel, draws, tiles),
        out_shape=(
            shape((factors, steps), f32),
            shape((draws + 1, factors), f32),
            shape((draws, LANES), f32),
        ),
        name="edge",
        compiler_params=room(3),
    )(innov, innov_scale.reshape(1, factors), spread, beyond, product)
    local_paths, running = pl.pallas_call(
        functools.partial(forward_kernel, draws, tiles),
        out_shape=(shape((draws, factors, steps), f32), shape((factors, steps), f32)),
        name="forward_scan",
        compiler_params=room(4),
    )(innov, decay_rate, weight)
    path_low = pl.pallas_call(
        functools.partial(enter_kernel, draws),
        out_shape=shape((draws, factors, steps), bf16),
        name="enter",
        compiler_params=room(2),
    )(local_paths, running, *carried(summary, draws + 1, False))

    pieces = [path_low] + [swap(path_low, "series", key) for key in range(1, parts)]
    noise = noise_scale.reshape(series // LANES, LANES)
    seen = returns.T
    loads = loadings.transpose(1, 0, 2)
    loads_t = loadings.transpose(1, 2, 0)
    rows = min(256, series // 2)
    body = draws * tiles * factors
    still = lambda dims: pl.BlockSpec(dims, lambda i: (0,) * len(dims))
    size = series * wide
    half, piece = size // 2, size // spans
    grads, load_share = pl.pallas_call(
        functools.partial(residual_kernel, draws, parts),
        out_shape=(
            shape((parts, body + TAIL, LANES), f32),
            shape((2, half + TAIL, LANES), f32),
        ),
        grid_spec=pl.GridSpec(
            grid=(series // rows,),
            in_specs=[still((draws, factors, steps))] * parts
            + [
                pl.BlockSpec((rows, steps), lambda i: (i, 0)),
                pl.BlockSpec((draws, rows, all_factors), lambda i: (0, i, 0)),
                pl.BlockSpec((draws, all_factors, rows), lambda i: (0, 0, i)),
                still((series // LANES, LANES)),
                still((draws, LANES)),
            ],
            out_specs=[
                still((parts, body + TAIL, LANES)),
                still((2, half + TAIL, LANES)),
            ],
            scratch_shapes=[
                pltpu.VMEM((draws, all_factors, steps), bf16),
                pltpu.VMEM((draws, LANES), f32),
                pltpu.VMEM((8, LANES), f32),
            ],
        ),
        name="residual",
        compiler_params=room(16),
    )(*pieces, seen, loads, loads_t, noise, squares)

    pick = lambda value, place: lax.dynamic_slice(value, (place, 0, 0), (1,) + value.shape[1:], allow_negative_indices=False)[0]
    sent = [pick(grads, place).astype(f16) for place in seats[1:]]
    arrived = [swap(value, "series", key + 1) for key, value in enumerate(sent)]

    chips = spans // 2
    whole = pl.BlockSpec(memory_space=pltpu.VMEM)
    other = swap(pick(load_share, far_core).astype(f16), "tm", 1).astype(f32)
    kept = pl.pallas_call(
        join_kernel,
        out_shape=shape((chips, piece + TAIL, LANES), f32),
        in_specs=[whole, whole],
        out_specs=whole,
        name="join",
        compiler_params=room(8),
    )(load_share, other)
    others = [swap(pick(kept, chips_at[key]).astype(f16), "tm", 2 * key).astype(f32) for key in range(1, chips)]
    total, factor = pl.pallas_call(
        functools.partial(total_kernel, float(math.ceil(math.log2(chips)))),
        out_shape=(shape((piece, LANES), f32), shape((1, LANES), f32)),
        in_specs=[whole] * chips,
        out_specs=(whole, whole),
        name="total",
        compiler_params=room(4),
    )(kept, *others)
    total = lax.optimization_barrier(total.astype(f16))
    totals = [total] + [swap(total, "tm", 2 * key) for key in range(1, chips)]
    mine = pl.pallas_call(
        assemble_kernel,
        out_shape=shape((half, LANES), f32),
        name="assemble",
        compiler_params=room(4),
    )(*[value.astype(f32) for value in totals])
    theirs = swap(mine.astype(f16), "tm", 1).astype(f32)
    grad_load = None
    for value, flip in ((mine, 0), (theirs, 1)):
        grad_load = write_half(value, factor, flip, grad_load, size)
    grad_load = grad_load.reshape(series, all_factors // LANES, draws, LANES).transpose(0, 2, 1, 3)
    grad_load = grad_load.reshape(series, draws, all_factors)

    path_grads, leaving = pl.pallas_call(
        functools.partial(gather_kernel, draws, tiles, parts),
        out_shape=(shape((body, LANES), f32), shape((2 * draws + 1, factors), f32)),
        name="gather",
        compiler_params=room(4),
    )(running, summary, grads, *[value.astype(f32) for value in arrived])
    local_adjoint, tail = pl.pallas_call(
        functools.partial(backward_kernel, draws, tiles),
        out_shape=(shape((draws, factors, steps), f32), shape((factors, steps), f32)),
        name="backward_scan",
        compiler_params=room(3),
    )(decay_rate, path_grads)
    grad_innov, density = pl.pallas_call(
        functools.partial(leave_kernel, draws, tiles),
        out_shape=(shape(innov.shape, f32), shape((draws, factors), f32)),
        name="leave",
        compiler_params=room(3),
    )(local_adjoint, tail, weight, innov, *carried(leaving, draws + 1, True))
    grad_innov = grad_innov.reshape(factors, tiles, draws, LANES).transpose(0, 2, 1, 3)
    grad_innov = grad_innov.reshape(factors, draws, steps)

    log_density = density[:, 0] / (spans * parts)
    return (grad_innov, grad_load, log_density)


def solution(mesh):
    placed = (
        P("tm", "series"),
        P("series", None, "tm"),
        P("series", "tm"),
        P("series"),
        P("series", None, None),
        P("series"),
    )

    return jax.shard_map(
        local,
        mesh=mesh,
        in_specs=placed,
        out_specs=(P("series", None, "tm"), P("series", None, None), P()),
        check_vma=False,
    )
```

```python
import functools
import math

import jax
import jax.numpy as jnp
from jax import lax
from jax.experimental import pallas as pl
from jax.experimental.pallas import tpu as pltpu
from jax.sharding import PartitionSpec as P


freedom = 5.0
LANES = 128
TAIL = 16
f32 = jnp.float32
bf16 = jnp.bfloat16
f16 = jnp.float16


def swap(value, axis, key):
    count = lax.axis_size(axis)
    return lax.ppermute(value, axis, [(i, i ^ key) for i in range(count)])


def eye(size):
    rows = lax.broadcasted_iota(jnp.int32, (size, size), 0)
    return rows == lax.broadcasted_iota(jnp.int32, (size, size), 1)


def to_column(row, same):
    return jnp.sum(jnp.where(same, row, 0.0), axis=1, keepdims=True)


def to_row(column, same):
    return jnp.sum(jnp.where(same, column, 0.0), axis=0, keepdims=True)


def tile_scan(decay, pushes, backward):
    lane = lax.broadcasted_iota(jnp.int32, decay.shape, 1)
    width = decay.shape[1]
    step = 1
    while step < width:
        turn = width - step if backward else step
        inside = lane < width - step if backward else lane >= step
        gate = jnp.where(inside, decay, 0.0)
        pushes = [p + gate * pltpu.roll(p, turn, 1) for p in pushes]
        decay = decay * jnp.where(inside, pltpu.roll(decay, turn, 1), 1.0)
        step *= 2
    return decay, pushes


def block_scan(decays, pushes, backward):
    tiles = len(decays)
    draws = len(pushes[0])
    order = range(tiles - 1, -1, -1) if backward else range(tiles)
    edge = slice(0, 1) if backward else slice(LANES - 1, LANES)
    run, out = [None] * tiles, [None] * tiles
    carry = None
    for j in order:
        a, b = tile_scan(decays[j], pushes[j], backward)
        if carry is not None:
            b = [b[d] + a * carry[1][d] for d in range(draws)]
            a = a * carry[0]
        run[j], out[j] = a, b
        carry = (a[:, edge], [x[:, edge] for x in b])
    return run, out, carry


def beyond_kernel(tiles, decay, spread, beyond, product, held):
    factors = decay.shape[0]
    held[...] = decay[...]
    lane = lax.broadcasted_iota(jnp.int32, (factors, LANES), 1)
    after = jnp.ones((factors, 1), f32)
    for j in range(tiles - 1, -1, -1):
        part = slice(j * LANES, (j + 1) * LANES)
        a = decay[:, part]
        spread[:, part] = jnp.sqrt((1.0 - a) * (1.0 + a))
        run, _ = tile_scan(a, [], True)
        beyond[:, part] = jnp.where(lane < LANES - 1, pltpu.roll(run, LANES - 1, 1), 1.0) * after
        after = after * run[:, 0:1]
    product[...] = to_row(after, eye(factors))


def edge_kernel(draws, tiles, innov, scale, spread, beyond, product, pushes, summary, squares):
    factors = spread.shape[0]
    same = eye(factors)
    column = to_column(scale[...], same)
    total = [jnp.zeros((factors, LANES), f32)] * draws
    ends = [jnp.zeros((factors, LANES), f32)] * draws
    for j in range(tiles):
        part = slice(j * LANES, (j + 1) * LANES)
        w = spread[:, part] * column
        for d in range(draws):
            x = innov[pl.ds(j * draws + d, factors, stride=tiles * draws), :]
            push = w * x
            pushes[d, :, part] = push
            total[d] = total[d] + x * x
            ends[d] = ends[d] + push * beyond[:, part]
    summary[0:1, :] = product[...]
    for d in range(draws):
        summary[d + 1:d + 2, :] = to_row(jnp.sum(ends[d], axis=1, keepdims=True), same)
        squares[d:d + 1, :] = jnp.sum(total[d], axis=0, keepdims=True)


def forward_kernel(draws, tiles, decay, pushed, local, running):
    parts = [slice(j * LANES, (j + 1) * LANES) for j in range(tiles)]
    decays = [decay[:, part] for part in parts]
    pushes = [[pushed[d, :, part] for d in range(draws)] for part in parts]
    run, out, _ = block_scan(decays, pushes, False)
    for j in range(tiles):
        running[:, j * LANES:(j + 1) * LANES] = run[j]
        for d in range(draws):
            local[d, :, j * LANES:(j + 1) * LANES] = out[j][d]


def seat(backward):
    count, mine = lax.axis_size("tm"), lax.axis_index("tm")
    return count - 1 - mine if backward else mine


def pair_kernel(rows, backward, bit, summary, other, whole):
    later = (seat(backward) // bit) % 2 == 1
    mine, theirs = summary[...], other[...]
    first, second = jnp.where(later, theirs, mine), jnp.where(later, mine, theirs)
    whole[0:1, :] = first[0:1] * second[0:1]
    whole[1:rows, :] = second[0:1] * first[1:rows] + second[1:rows]
    if rows < mine.shape[0]:
        whole[rows:, :] = first[rows:] + second[rows:]


def entered(rows, backward, other, totals):
    mine = seat(backward)
    later, pair, pairs = mine % 2 == 1, mine // 2, len(totals)
    theirs = other[...]
    values = [total[...] for total in totals]
    entering = jnp.zeros_like(theirs[1:rows])
    summed = jnp.zeros_like(theirs[rows:]) if rows < theirs.shape[0] else None
    for place in range(pairs):
        here = values[0]
        for key in range(1, pairs):
            here = jnp.where((pair ^ key) == place, values[key], here)
        entering = jnp.where(place < pair, here[0:1] * entering + here[1:rows], entering)
        if summed is not None:
            summed = summed + here[rows:]
    return jnp.where(later, theirs[0:1] * entering + theirs[1:rows], entering), summed


def enter_kernel(draws, local, running, other, *refs):
    totals, path = refs[:-1], refs[-1]
    same = eye(running.shape[0])
    entering, _ = entered(draws + 1, False, other, totals)
    for d in range(draws):
        column = to_column(entering[d:d + 1, :], same)
        path[d] = (local[d] + running[...] * column).astype(bf16)


def residual_kernel(draws, parts, *refs):
    pieces, (returns, loads, loads_t, noise, squares, grads, shares, paths, density, top) = refs[:parts], refs[parts:]
    factors = pieces[0].shape[1]
    step = pl.program_id(0)
    count = pl.num_programs(0)
    wide = paths.shape[1] // LANES
    side = step // (count // 2)
    base = (step % (count // 2)) * (returns.shape[1] * wide * draws)

    @pl.when(step == 0)
    def _():
        for n in range(parts):
            start = pl.multiple_of((lax.axis_index("series") ^ n) * factors, factors)
            paths[:, pl.ds(start, factors), :] = pieces[n][...]
        grads[...] = jnp.zeros_like(grads)
        density[...] = jnp.zeros_like(density)
        top[...] = jnp.zeros_like(top)

    seen = returns[...].T.astype(f32)
    rows = seen.shape[0]
    same = eye(LANES)
    groups = rows // LANES
    spread = [to_column(noise[pl.ds(step * groups + g, 1), :], same) for g in range(groups)]
    spread = jnp.concatenate(spread, axis=0)
    s2 = freedom * (spread * spread)
    inverse = 1.0 / s2
    tiles = seen.shape[1] // LANES
    half = rows // 2
    for d in range(draws):
        fitted = jnp.dot(loads[d], paths[d], preferred_element_type=f32)
        residual = seen - fitted
        square = residual * residual
        pulled = ((freedom + 1.0) * residual / (s2 + square)).astype(bf16)
        ratio = square * inverse
        first, second = ratio[:half], ratio[half:]
        both = jnp.log1p(first + second * (1.0 + first))
        both = jnp.sum(both, axis=0, keepdims=True)
        lanes = both[:, :LANES]
        for j in range(1, both.shape[1] // LANES):
            lanes = lanes + both[:, j * LANES:(j + 1) * LANES]
        density[d:d + 1, :] += lanes
        product = jnp.dot(loads_t[d], pulled, preferred_element_type=f32)
        for n in range(parts):
            for j in range(tiles):
                to = slice((d * tiles + j) * factors, (d * tiles + j + 1) * factors)
                grads[n, to, :] += product[n * factors:(n + 1) * factors, j * LANES:(j + 1) * LANES]
        share = lax.dot_general(pulled, paths[d], (((1,), (1,)), ((), ())), preferred_element_type=f32)
        most = top[...]
        for j in range(wide):
            tile = share[:, j * LANES:(j + 1) * LANES]
            shares[side, pl.ds(base + (j * draws + d), rows, stride=wide * draws), :] = tile
            most = jnp.maximum(most, jnp.max(jnp.abs(tile).reshape(rows // 8, 8, LANES), axis=0))
        top[...] = most

    @pl.when(step == pl.num_programs(0) - 1)
    def _():
        body = draws * tiles * factors
        cells = pl.num_programs(0) * rows * seen.shape[1]
        peak = jnp.zeros((1, LANES), f32)
        for n in range(parts):
            peak = jnp.maximum(peak, jnp.max(jnp.abs(grads[n, :body, :]), axis=0, keepdims=True))
        level = exponent(peak)
        tail = [level]
        for d in range(draws):
            value = -(freedom + 1.0) * 0.5 * density[d:d + 1, :] - 0.5 * squares[d:d + 1, :]
            tail += coded(jnp.sum(value, axis=1, keepdims=True) * (1.0 / cells))
        tail = stacked(tail)
        factor = jnp.exp2(15.0 - level)
        for n in range(parts):
            grads[n, :body, :] = grads[n, :body, :] * factor
            grads[n, body:, :] = tail
        half = shares.shape[1] - TAIL
        level = exponent(jnp.max(top[...], axis=0, keepdims=True))
        factor = jnp.exp2(15.0 - level)
        for n in range(2):
            shares[n, :half, :] = shares[n, :half, :] * factor
            shares[n, half:, :] = stacked([level])


def coded(value):
    value = jnp.broadcast_to(value, (1, LANES))
    level = exponent(jnp.abs(value))
    left = value * jnp.exp2(-level)
    codes = [level]
    unit = 1024.0
    for _ in range(3):
        code = (left * unit + 12582912.0) - 12582912.0
        codes.append(code)
        left = left - code * (1.0 / unit)
        unit = unit * 1024.0
    return codes


def decoded(rows):
    level, first, second, third = [rows[n:n + 1, :] for n in range(4)]
    small = 1.0 / 1024.0
    return jnp.exp2(level) * (first + (second + third * small) * small) * small


def stacked(rows):
    place = lax.broadcasted_iota(jnp.int32, (TAIL, LANES), 0)
    out = jnp.zeros((TAIL, LANES), f32)
    for n, row in enumerate(rows):
        out = jnp.where(place == n, row, out)
    return out


def exponent(lanes):
    top = jnp.maximum(jnp.max(lanes, axis=1, keepdims=True), 1e-30)
    return jnp.broadcast_to(jnp.ceil(jnp.log(top) * (1.0 / math.log(2.0))), lanes.shape)


def join_kernel(mine, other, out):
    core = lax.axis_index("tm") % 2
    body = other.shape[0] - TAIL
    chips = out.shape[0]
    piece = body // chips
    own, far = mine[core, body:body + 1, :], other[body:body + 1, :]
    level = jnp.maximum(own, far) + 1.0
    own, far = jnp.exp2(own - level), jnp.exp2(far - level)
    for n in range(chips):
        rows = slice(n * piece, (n + 1) * piece)
        out[n, :piece, :] = mine[core, rows, :] * own + other[rows, :] * far
        out[n, piece:, :] = stacked([level])


def total_kernel(lift, mine, *refs):
    others, (out, factor) = refs[:-2], refs[-2:]
    piece = out.shape[0]
    here = lax.axis_index("tm") // 2
    levels = [mine[here, piece:piece + 1, :]] + [other[piece:piece + 1, :] for other in others]
    top = levels[0]
    for level in levels[1:]:
        top = jnp.maximum(top, level)
    top = top + lift
    total = mine[here, :piece, :] * jnp.exp2(levels[0] - top)
    for level, other in zip(levels[1:], others):
        total = total + other[:piece, :] * jnp.exp2(level - top)
    out[...] = total
    factor[...] = jnp.exp2(top - 15.0)


def gather_kernel(draws, tiles, parts, running, products, mine, *refs):
    others, (gathered, summary) = refs[:-2], refs[-2:]
    factors = running.shape[0]
    body = draws * tiles * factors
    here = lax.axis_index("series")
    tails = [mine[here, body:, :]] + [other[body:, :] for other in others]
    scales = [jnp.exp2(rows[0:1, :] - 15.0) for rows in tails]
    same = eye(factors)
    summary[0:1, :] = products[0:1, :]
    for d in range(draws):
        known = [decoded(rows[1 + 4 * d:5 + 4 * d, :]) for rows in tails]
        density = jnp.zeros((1, LANES), f32)
        for place in range(parts):
            for n in range(parts):
                density = density + jnp.where((here ^ n) == place, known[n], 0.0)
        summary[draws + 1 + d:draws + 2 + d, :] = density[:, :factors]
        leaving = jnp.zeros((factors, LANES), f32)
        for j in range(tiles):
            rows = slice((d * tiles + j) * factors, (d * tiles + j + 1) * factors)
            value = mine[here, rows, :] * scales[0]
            for other, scale in zip(others, scales[1:]):
                value = value + other[rows, :] * scale
            gathered[rows, :] = value
            leaving = leaving + value * running[:, j * LANES:(j + 1) * LANES]
        summary[d + 1:d + 2, :] = to_row(jnp.sum(leaving, axis=1, keepdims=True), same)


def backward_kernel(draws, tiles, decay, grads, local, tail):
    factors = decay.shape[0]
    lane = lax.broadcasted_iota(jnp.int32, (factors, LANES), 1)
    decays, pushes = [], []
    for j in range(tiles):
        a = decay[:, j * LANES:(j + 1) * LANES]
        if j + 1 < tiles:
            after = decay[:, (j + 1) * LANES:(j + 2) * LANES][:, 0:1]
        else:
            after = jnp.ones((factors, 1), f32)
        decays.append(jnp.where(lane < LANES - 1, pltpu.roll(a, LANES - 1, 1), after))
        rows = lambda d: slice((d * tiles + j) * factors, (d * tiles + j + 1) * factors)
        pushes.append([grads[rows(d), :] for d in range(draws)])
    run, out, _ = block_scan(decays, pushes, True)
    for j in range(tiles):
        tail[:, j * LANES:(j + 1) * LANES] = run[j]
        for d in range(draws):
            local[d, :, j * LANES:(j + 1) * LANES] = out[j][d]


def leave_kernel(draws, tiles, cells, local, tail, decay, scale, innov, value, *refs):
    climb, (out, density, far, sem) = refs[:-4], refs[-4:]
    half = value.shape[0]
    move = pltpu.make_async_copy(value, far.at[pl.ds(pl.multiple_of((lax.axis_index("tm") % 2) * half, half), half), :], sem)
    move.start()
    factors = tail.shape[0]
    same = eye(factors)
    arriving, summed = entered(draws + 1, True, climb[0], climb[1:])
    sized = to_column(scale[...], same)
    columns = [to_column(arriving[d:d + 1, :], same) for d in range(draws)]
    for d in range(draws):
        density[d] = jnp.max(summed[d:d + 1, :]) * (1.0 / cells)
    for j in range(tiles):
        part = slice(j * LANES, (j + 1) * LANES)
        a = decay[:, part]
        weight = jnp.sqrt((1.0 - a) * (1.0 + a)) * sized
        for d in range(draws):
            rows = pl.ds(j * draws + d, factors, stride=tiles * draws)
            adjoint = local[d, :, part] + tail[:, part] * columns[d]
            out[rows, :] = weight * adjoint - innov[rows, :]
    move.wait()


def room(mebibytes):
    return pltpu.CompilerParams(vmem_limit_bytes=mebibytes << 20)


def assemble_kernel(*refs):
    pieces, out = refs[:-1], refs[-1]
    rows = pieces[0].shape[0]
    for key, piece in enumerate(pieces):
        start = pl.multiple_of(((lax.axis_index("tm") // 2) ^ key) * rows, rows)
        out[pl.ds(start, rows), :] = piece[...]


def write_kernel(flip, value, *refs):
    out, sem = refs[-2:]
    half = value.shape[0]
    move = pltpu.make_async_copy(value, out.at[pl.ds(pl.multiple_of(((lax.axis_index("tm") + flip) % 2) * half, half), half), :], sem)
    move.start()
    move.wait()


def write_half(value, flip, out, size):
    far = pl.BlockSpec(memory_space=pltpu.HBM)
    specs = [pl.BlockSpec(memory_space=pltpu.VMEM)]
    return pl.pallas_call(
        functools.partial(write_kernel, flip),
        out_shape=shape((size, LANES), f32),
        in_specs=specs if out is None else specs + [far],
        out_specs=far,
        input_output_aliases={} if out is None else {1: 0},
        scratch_shapes=[pltpu.SemaphoreType.DMA],
        name="write_half",
        compiler_params=room(4),
    )(value, *([] if out is None else [out]))


def shape(dims, kind):
    return jax.ShapeDtypeStruct(dims, kind)


def carried(summary, rows, backward):
    pairs = lax.axis_size("tm") // 2
    other = swap(summary, "tm", 1)
    whole = pl.pallas_call(
        functools.partial(pair_kernel, rows, backward, 1),
        out_shape=shape(summary.shape, f32),
        compiler_params=room(1),
    )(summary, other)
    return [other, whole] + [swap(whole, "tm", 2 * key) for key in range(1, pairs)]


def local(returns, innovations, decay_rate, innov_scale, loadings, noise_scale):
    factors, draws, steps = innovations.shape
    series = returns.shape[1]
    parts, spans = lax.axis_size("series"), lax.axis_size("tm")
    where, when = lax.axis_index("series"), lax.axis_index("tm")
    tiles = steps // LANES
    all_factors = factors * parts
    wide = all_factors * draws // LANES

    innov = innovations.reshape(factors, draws, tiles, LANES).transpose(0, 2, 1, 3)
    innov = innov.reshape(factors * tiles * draws, LANES)
    numbers = [where ^ key for key in range(parts)] + [1 - when % 2]
    numbers += [(when // 2) ^ key for key in range(spans // 2)]
    decay_rate, numbers = lax.optimization_barrier((decay_rate, numbers))
    seats, far_core = numbers[:parts], numbers[parts]
    chips_at = numbers[parts + 1:]
    spread, beyond, product, decays = pl.pallas_call(
        functools.partial(beyond_kernel, tiles),
        out_shape=(
            shape((factors, steps), f32),
            shape((factors, steps), f32),
            shape((1, factors), f32),
            shape((factors, steps), f32),
        ),
        name="beyond",
        cost_estimate=pl.CostEstimate(flops=2_000_000_000, bytes_accessed=1 << 20, transcendentals=0),
        compiler_params=room(2),
    )(decay_rate)
    pushes, summary, squares = pl.pallas_call(
        functools.partial(edge_kernel, draws, tiles),
        out_shape=(
            shape((draws, factors, steps), f32),
            shape((draws + 1, factors), f32),
            shape((draws, LANES), f32),
        ),
        name="edge",
        compiler_params=room(3),
    )(innov, innov_scale.reshape(1, factors), spread, beyond, product)
    local_paths, running = pl.pallas_call(
        functools.partial(forward_kernel, draws, tiles),
        out_shape=(shape((draws, factors, steps), f32), shape((factors, steps), f32)),
        name="forward_scan",
        compiler_params=room(4),
    )(decays, pushes)
    path_low = pl.pallas_call(
        functools.partial(enter_kernel, draws),
        out_shape=shape((draws, factors, steps), bf16),
        name="enter",
        compiler_params=room(2),
    )(local_paths, running, *carried(summary, draws + 1, False))

    pieces = [path_low] + [swap(path_low, "series", key) for key in range(1, parts)]
    noise = noise_scale.reshape(series // LANES, LANES)
    loads = loadings.transpose(1, 0, 2)
    loads_t = loadings.transpose(1, 2, 0)
    rows = min(256, series // 2)
    body = draws * tiles * factors
    still = lambda dims: pl.BlockSpec(dims, lambda i: (0,) * len(dims))
    size = series * wide
    half, piece = size // 2, size // spans
    grads, load_share = pl.pallas_call(
        functools.partial(residual_kernel, draws, parts),
        out_shape=(
            shape((parts, body + TAIL, LANES), f32),
            shape((2, half + TAIL, LANES), f32),
        ),
        grid_spec=pl.GridSpec(
            grid=(series // rows,),
            in_specs=[still((draws, factors, steps))] * parts
            + [
                pl.BlockSpec((steps, rows), lambda i: (0, i)),
                pl.BlockSpec((draws, rows, all_factors), lambda i: (0, i, 0)),
                pl.BlockSpec((draws, all_factors, rows), lambda i: (0, 0, i)),
                still((series // LANES, LANES)),
                still((draws, LANES)),
            ],
            out_specs=[
                still((parts, body + TAIL, LANES)),
                still((2, half + TAIL, LANES)),
            ],
            scratch_shapes=[
                pltpu.VMEM((draws, all_factors, steps), bf16),
                pltpu.VMEM((draws, LANES), f32),
                pltpu.VMEM((8, LANES), f32),
            ],
        ),
        name="residual",
        compiler_params=room(16),
    )(*pieces, returns, loads, loads_t, noise, squares)

    pick = lambda value, place: lax.dynamic_slice(value, (place, 0, 0), (1,) + value.shape[1:], allow_negative_indices=False)[0]
    sent = [pick(grads, place).astype(f16) for place in seats[1:]]
    arrived = [swap(value, "series", key) for key, value in enumerate(sent, 1)]

    chips = spans // 2
    whole = pl.BlockSpec(memory_space=pltpu.VMEM)
    other = swap(pick(load_share, far_core).astype(f16), "tm", 1).astype(f32)
    kept = pl.pallas_call(
        join_kernel,
        out_shape=shape((chips, piece + TAIL, LANES), f32),
        in_specs=[whole, whole],
        out_specs=whole,
        name="join",
        compiler_params=room(8),
    )(load_share, other)
    others = [swap(pick(kept, chips_at[key]).astype(f16), "tm", 2 * key).astype(f32) for key in range(1, chips)]
    total, factor = pl.pallas_call(
        functools.partial(total_kernel, float(math.ceil(math.log2(chips)))),
        out_shape=(shape((piece, LANES), f32), shape((1, LANES), f32)),
        in_specs=[whole] * chips,
        out_specs=(whole, whole),
        name="total",
        compiler_params=room(4),
    )(kept, *others)
    total = lax.optimization_barrier(total.astype(f16))
    totals = [total] + [swap(total, "tm", 2 * key) for key in range(1, chips)]
    mine = pl.pallas_call(
        assemble_kernel,
        out_shape=shape((half, LANES), f32),
        name="assemble",
        compiler_params=room(4),
    )(*[value.astype(f32) for value in totals])
    theirs = swap(mine.astype(f16), "tm", 1).astype(f32) * factor
    path_grads, leaving = pl.pallas_call(
        functools.partial(gather_kernel, draws, tiles, parts),
        out_shape=(shape((body, LANES), f32), shape((2 * draws + 1, factors), f32)),
        name="gather",
        compiler_params=room(4),
    )(running, summary, grads, *[value.astype(f32) for value in arrived])
    local_adjoint, tail = pl.pallas_call(
        functools.partial(backward_kernel, draws, tiles),
        out_shape=(shape((draws, factors, steps), f32), shape((factors, steps), f32)),
        name="backward_scan",
        compiler_params=room(3),
    )(decays, path_grads)
    climb = carried(leaving, draws + 1, True)
    grad_innov, log_density, grad_load = pl.pallas_call(
        functools.partial(leave_kernel, draws, tiles, float(spans * parts)),
        out_shape=(shape(innov.shape, f32), shape((draws,), f32), shape((size, LANES), f32)),
        in_specs=[whole] * (6 + len(climb)),
        out_specs=(whole, pl.BlockSpec(memory_space=pltpu.SMEM), pl.BlockSpec(memory_space=pltpu.HBM)),
        scratch_shapes=[pltpu.SemaphoreType.DMA],
        name="leave",
        compiler_params=room(4),
    )(local_adjoint, tail, decays, innov_scale.reshape(1, factors), innov, mine * factor, *climb)
    grad_load = write_half(theirs, 1, grad_load, size)
    grad_load = grad_load.reshape(series, all_factors // LANES, draws, LANES).transpose(0, 2, 1, 3)
    grad_load = grad_load.reshape(series, draws, all_factors)
    grad_innov = grad_innov.reshape(factors, tiles, draws, LANES).transpose(0, 2, 1, 3)
    grad_innov = grad_innov.reshape(factors, draws, steps)

    return (grad_innov, grad_load, log_density)


def solution(mesh):
    placed = (
        P("tm", "series"),
        P("series", None, "tm"),
        P("series", "tm"),
        P("series"),
        P("series", None, None),
        P("series"),
    )

    return jax.shard_map(
        local,
        mesh=mesh,
        in_specs=placed,
        out_specs=(P("series", None, "tm"), P("series", None, None), P()),
        check_vma=False,
    )
```

```python
import functools
import math

import jax
import jax.numpy as jnp
from jax import lax
from jax.experimental import pallas as pl
from jax.experimental.pallas import tpu as pltpu
from jax.sharding import PartitionSpec as P


freedom = 5.0
LANES = 128
TAIL = 16
f32 = jnp.float32
bf16 = jnp.bfloat16
f16 = jnp.float16


def swap(value, axis, key):
    count = lax.axis_size(axis)
    return lax.ppermute(value, axis, [(i, i ^ key) for i in range(count)])


def eye(size):
    rows = lax.broadcasted_iota(jnp.int32, (size, size), 0)
    return rows == lax.broadcasted_iota(jnp.int32, (size, size), 1)


def to_column(row, same):
    return jnp.sum(jnp.where(same, row, 0.0), axis=1, keepdims=True)


def to_row(column, same):
    return jnp.sum(jnp.where(same, column, 0.0), axis=0, keepdims=True)


def tile_scan(decay, pushes, backward):
    lane = lax.broadcasted_iota(jnp.int32, decay.shape, 1)
    width = decay.shape[1]
    step = 1
    while step < width:
        turn = width - step if backward else step
        inside = lane < width - step if backward else lane >= step
        gate = jnp.where(inside, decay, 0.0)
        pushes = [p + gate * pltpu.roll(p, turn, 1) for p in pushes]
        decay = decay * jnp.where(inside, pltpu.roll(decay, turn, 1), 1.0)
        step *= 2
    return decay, pushes


def block_scan(decays, pushes, backward):
    tiles = len(decays)
    draws = len(pushes[0])
    order = range(tiles - 1, -1, -1) if backward else range(tiles)
    edge = slice(0, 1) if backward else slice(LANES - 1, LANES)
    run, out = [None] * tiles, [None] * tiles
    carry = None
    for j in order:
        a, b = tile_scan(decays[j], pushes[j], backward)
        if carry is not None:
            b = [b[d] + a * carry[1][d] for d in range(draws)]
            a = a * carry[0]
        run[j], out[j] = a, b
        carry = (a[:, edge], [x[:, edge] for x in b])
    return run, out, carry


def beyond_kernel(tiles, decay, spread, beyond, product, held):
    factors = decay.shape[0]
    held[...] = decay[...]
    lane = lax.broadcasted_iota(jnp.int32, (factors, LANES), 1)
    after = jnp.ones((factors, 1), f32)
    for j in range(tiles - 1, -1, -1):
        part = slice(j * LANES, (j + 1) * LANES)
        a = decay[:, part]
        spread[:, part] = jnp.sqrt((1.0 - a) * (1.0 + a))
        run, _ = tile_scan(a, [], True)
        beyond[:, part] = jnp.where(lane < LANES - 1, pltpu.roll(run, LANES - 1, 1), 1.0) * after
        after = after * run[:, 0:1]
    product[...] = to_row(after, eye(factors))


def edge_kernel(draws, tiles, innov, scale, spread, beyond, product, pushes, summary, squares):
    factors = spread.shape[0]
    same = eye(factors)
    column = to_column(scale[...], same)
    total = [jnp.zeros((factors, LANES), f32)] * draws
    ends = [jnp.zeros((factors, LANES), f32)] * draws
    for j in range(tiles):
        part = slice(j * LANES, (j + 1) * LANES)
        w = spread[:, part] * column
        for d in range(draws):
            x = innov[pl.ds(j * draws + d, factors, stride=tiles * draws), :]
            push = w * x
            pushes[d, :, part] = push
            total[d] = total[d] + x * x
            ends[d] = ends[d] + push * beyond[:, part]
    summary[0:1, :] = product[...]
    for d in range(draws):
        summary[d + 1:d + 2, :] = to_row(jnp.sum(ends[d], axis=1, keepdims=True), same)
        squares[d:d + 1, :] = jnp.sum(total[d], axis=0, keepdims=True)


def forward_kernel(draws, tiles, decay, pushed, local, running):
    parts = [slice(j * LANES, (j + 1) * LANES) for j in range(tiles)]
    decays = [decay[:, part] for part in parts]
    pushes = [[pushed[d, :, part] for d in range(draws)] for part in parts]
    run, out, _ = block_scan(decays, pushes, False)
    for j in range(tiles):
        running[:, j * LANES:(j + 1) * LANES] = run[j]
        for d in range(draws):
            local[d, :, j * LANES:(j + 1) * LANES] = out[j][d]


def seat(backward):
    count, mine = lax.axis_size("tm"), lax.axis_index("tm")
    return count - 1 - mine if backward else mine


def pair_kernel(rows, backward, bit, summary, other, whole):
    later = (seat(backward) // bit) % 2 == 1
    mine, theirs = summary[...], other[...]
    first, second = jnp.where(later, theirs, mine), jnp.where(later, mine, theirs)
    whole[0:1, :] = first[0:1] * second[0:1]
    whole[1:rows, :] = second[0:1] * first[1:rows] + second[1:rows]
    if rows < mine.shape[0]:
        whole[rows:, :] = first[rows:] + second[rows:]


def entered(rows, backward, other, totals):
    mine = seat(backward)
    later, pair, pairs = mine % 2 == 1, mine // 2, len(totals)
    theirs = other[...]
    values = [total[...] for total in totals]
    entering = jnp.zeros_like(theirs[1:rows])
    summed = jnp.zeros_like(theirs[rows:]) if rows < theirs.shape[0] else None
    for place in range(pairs):
        here = values[0]
        for key in range(1, pairs):
            here = jnp.where((pair ^ key) == place, values[key], here)
        entering = jnp.where(place < pair, here[0:1] * entering + here[1:rows], entering)
        if summed is not None:
            summed = summed + here[rows:]
    return jnp.where(later, theirs[0:1] * entering + theirs[1:rows], entering), summed


def enter_kernel(draws, local, running, other, *refs):
    totals, path = refs[:-1], refs[-1]
    same = eye(running.shape[0])
    entering, _ = entered(draws + 1, False, other, totals)
    for d in range(draws):
        column = to_column(entering[d:d + 1, :], same)
        path[d] = (local[d] + running[...] * column).astype(bf16)


def residual_kernel(draws, parts, *refs):
    pieces, (returns, loads, loads_t, noise, squares, grads, shares, paths, density, top) = refs[:parts], refs[parts:]
    factors = pieces[0].shape[1]
    step = pl.program_id(0)
    count = pl.num_programs(0)
    wide = paths.shape[1] // LANES
    side = step // (count // 2)
    base = (step % (count // 2)) * (returns.shape[1] * wide * draws)

    @pl.when(step == 0)
    def _():
        for n in range(parts):
            start = pl.multiple_of((lax.axis_index("series") ^ n) * factors, factors)
            paths[:, pl.ds(start, factors), :] = pieces[n][...]
        grads[...] = jnp.zeros_like(grads)
        density[...] = jnp.zeros_like(density)
        top[...] = jnp.zeros_like(top)

    seen = returns[...].T.astype(f32)
    rows = seen.shape[0]
    same = eye(LANES)
    groups = rows // LANES
    spread = [to_column(noise[pl.ds(step * groups + g, 1), :], same) for g in range(groups)]
    spread = jnp.concatenate(spread, axis=0)
    s2 = freedom * (spread * spread)
    inverse = 1.0 / s2
    tiles = seen.shape[1] // LANES
    half = rows // 2
    for d in range(draws):
        fitted = jnp.dot(loads[d], paths[d], preferred_element_type=f32)
        residual = seen - fitted
        square = residual * residual
        pulled = ((freedom + 1.0) * residual / (s2 + square)).astype(bf16)
        ratio = square * inverse
        first, second = ratio[:half], ratio[half:]
        both = jnp.log1p(first + second * (1.0 + first))
        both = jnp.sum(both, axis=0, keepdims=True)
        lanes = both[:, :LANES]
        for j in range(1, both.shape[1] // LANES):
            lanes = lanes + both[:, j * LANES:(j + 1) * LANES]
        density[d:d + 1, :] += lanes
        product = jnp.dot(loads_t[d], pulled, preferred_element_type=f32)
        for n in range(parts):
            for j in range(tiles):
                to = slice((d * tiles + j) * factors, (d * tiles + j + 1) * factors)
                grads[n, to, :] += product[n * factors:(n + 1) * factors, j * LANES:(j + 1) * LANES]
        share = lax.dot_general(pulled, paths[d], (((1,), (1,)), ((), ())), preferred_element_type=f32)
        most = top[...]
        for j in range(wide):
            tile = share[:, j * LANES:(j + 1) * LANES]
            shares[side, pl.ds(base + (j * draws + d), rows, stride=wide * draws), :] = tile
            most = jnp.maximum(most, jnp.max(jnp.abs(tile).reshape(rows // 8, 8, LANES), axis=0))
        top[...] = most

    @pl.when(step == pl.num_programs(0) - 1)
    def _():
        body = draws * tiles * factors
        cells = pl.num_programs(0) * rows * seen.shape[1]
        peak = jnp.zeros((1, LANES), f32)
        for n in range(parts):
            peak = jnp.maximum(peak, jnp.max(jnp.abs(grads[n, :body, :]), axis=0, keepdims=True))
        level = exponent(peak)
        tail = [level]
        for d in range(draws):
            value = -(freedom + 1.0) * 0.5 * density[d:d + 1, :] - 0.5 * squares[d:d + 1, :]
            tail += coded(jnp.sum(value, axis=1, keepdims=True) * (1.0 / cells))
        tail = stacked(tail)
        factor = jnp.exp2(15.0 - level)
        for n in range(parts):
            grads[n, :body, :] = grads[n, :body, :] * factor
            grads[n, body:, :] = tail
        half = shares.shape[1] - TAIL
        level = exponent(jnp.max(top[...], axis=0, keepdims=True))
        factor = jnp.exp2(15.0 - level)
        for n in range(2):
            shares[n, :half, :] = shares[n, :half, :] * factor
            shares[n, half:, :] = stacked([level])


def coded(value):
    value = jnp.broadcast_to(value, (1, LANES))
    level = exponent(jnp.abs(value))
    left = value * jnp.exp2(-level)
    codes = [level]
    unit = 1024.0
    for _ in range(3):
        code = (left * unit + 12582912.0) - 12582912.0
        codes.append(code)
        left = left - code * (1.0 / unit)
        unit = unit * 1024.0
    return codes


def decoded(rows):
    level, first, second, third = [rows[n:n + 1, :] for n in range(4)]
    small = 1.0 / 1024.0
    return jnp.exp2(level) * (first + (second + third * small) * small) * small


def stacked(rows):
    place = lax.broadcasted_iota(jnp.int32, (TAIL, LANES), 0)
    out = jnp.zeros((TAIL, LANES), f32)
    for n, row in enumerate(rows):
        out = jnp.where(place == n, row, out)
    return out


def exponent(lanes):
    top = jnp.maximum(jnp.max(lanes, axis=1, keepdims=True), 1e-30)
    return jnp.broadcast_to(jnp.ceil(jnp.log(top) * (1.0 / math.log(2.0))), lanes.shape)


def join_kernel(mine, other, out):
    core = lax.axis_index("tm") % 2
    body = other.shape[0] - TAIL
    chips = out.shape[0]
    piece = body // chips
    own, far = mine[core, body:body + 1, :], other[body:body + 1, :]
    level = jnp.maximum(own, far) + 1.0
    own, far = jnp.exp2(own - level), jnp.exp2(far - level)
    for n in range(chips):
        rows = slice(n * piece, (n + 1) * piece)
        out[n, :piece, :] = mine[core, rows, :] * own + other[rows, :] * far
        out[n, piece:, :] = stacked([level])


def total_kernel(lift, mine, *refs):
    others, (out, factor) = refs[:-2], refs[-2:]
    piece = out.shape[0]
    here = lax.axis_index("tm") // 2
    levels = [mine[here, piece:piece + 1, :]] + [other[piece:piece + 1, :] for other in others]
    top = levels[0]
    for level in levels[1:]:
        top = jnp.maximum(top, level)
    top = top + lift
    total = mine[here, :piece, :] * jnp.exp2(levels[0] - top)
    for level, other in zip(levels[1:], others):
        total = total + other[:piece, :] * jnp.exp2(level - top)
    out[...] = total
    factor[...] = jnp.exp2(top - 15.0)


def gather_kernel(draws, tiles, parts, running, products, mine, *refs):
    others, (gathered, summary) = refs[:-2], refs[-2:]
    factors = running.shape[0]
    body = draws * tiles * factors
    here = lax.axis_index("series")
    tails = [mine[here, body:, :]] + [other[body:, :] for other in others]
    scales = [jnp.exp2(rows[0:1, :] - 15.0) for rows in tails]
    same = eye(factors)
    summary[0:1, :] = products[0:1, :]
    for d in range(draws):
        known = [decoded(rows[1 + 4 * d:5 + 4 * d, :]) for rows in tails]
        density = jnp.zeros((1, LANES), f32)
        for place in range(parts):
            for n in range(parts):
                density = density + jnp.where((here ^ n) == place, known[n], 0.0)
        summary[draws + 1 + d:draws + 2 + d, :] = density[:, :factors]
        leaving = jnp.zeros((factors, LANES), f32)
        for j in range(tiles):
            rows = slice((d * tiles + j) * factors, (d * tiles + j + 1) * factors)
            value = mine[here, rows, :] * scales[0]
            for other, scale in zip(others, scales[1:]):
                value = value + other[rows, :] * scale
            gathered[rows, :] = value
            leaving = leaving + value * running[:, j * LANES:(j + 1) * LANES]
        summary[d + 1:d + 2, :] = to_row(jnp.sum(leaving, axis=1, keepdims=True), same)


def unwind_kernel(tiles, decay, scale, gates, inner, weight, fade):
    factors = decay.shape[0]
    lane = lax.broadcasted_iota(jnp.int32, (factors, LANES), 1)
    sized = to_column(scale[...], eye(factors))
    beyond = jnp.ones((factors, 1), f32)
    for j in range(tiles - 1, -1, -1):
        part = slice(j * LANES, (j + 1) * LANES)
        a = decay[:, part]
        w = jnp.sqrt((1.0 - a) * (1.0 + a)) * sized
        weight[:, part] = w
        if j + 1 < tiles:
            after = decay[:, (j + 1) * LANES:(j + 2) * LANES][:, 0:1]
        else:
            after = jnp.ones((factors, 1), f32)
        run = jnp.where(lane < LANES - 1, pltpu.roll(a, LANES - 1, 1), after)
        for level in range(gates.shape[0]):
            step = 1 << level
            inside = lane < LANES - step
            gates[level, :, part] = jnp.where(inside, run, 0.0)
            run = run * jnp.where(inside, pltpu.roll(run, LANES - step, 1), 1.0)
        inner[:, part] = run
        fade[:, part] = w * run * beyond
        beyond = beyond * run[:, 0:1]


def backward_kernel(draws, tiles, gates, inner, grads, local):
    factors = inner.shape[0]
    carry = None
    for j in range(tiles - 1, -1, -1):
        part = slice(j * LANES, (j + 1) * LANES)
        rows = lambda d: slice((d * tiles + j) * factors, (d * tiles + j + 1) * factors)
        values = [grads[rows(d), :] for d in range(draws)]
        for level in range(gates.shape[0]):
            gate = gates[level, :, part]
            values = [p + gate * pltpu.roll(p, LANES - (1 << level), 1) for p in values]
        if carry is not None:
            values = [values[d] + inner[:, part] * carry[d] for d in range(draws)]
        for d in range(draws):
            local[d, :, part] = values[d]
        carry = [p[:, 0:1] for p in values]


def leave_kernel(draws, tiles, cells, count, *refs):
    pieces, refs = refs[:count], refs[count:]
    (local, fade, weight, innov), climb, (near, density, far, out, sems) = refs[:4], refs[4:-5], refs[-5:]
    lines, chips = pieces[0].shape[0], count // 2
    mine = lax.axis_index("tm")
    moves = []
    for n, piece in enumerate(pieces):
        side = (mine + n // chips) % 2
        start = pl.multiple_of((side * chips + ((mine // 2) ^ (n % chips))) * lines, lines)
        moves.append(pltpu.make_async_copy(piece, far.at[pl.ds(start, lines), :], sems.at[n]))
    for move in moves:
        move.start()
    factors = fade.shape[0]
    same = eye(factors)
    arriving, summed = entered(draws + 1, True, climb[0], climb[1:])
    columns = [to_column(arriving[d:d + 1, :], same) for d in range(draws)]
    for d in range(draws):
        density[d] = jnp.max(summed[d:d + 1, :]) * (1.0 / cells)
    for j in range(tiles):
        part = slice(j * LANES, (j + 1) * LANES)
        for d in range(draws):
            rows = pl.ds(j * draws + d, factors, stride=tiles * draws)
            out[rows, :] = weight[:, part] * local[d, :, part] + fade[:, part] * columns[d] - innov[rows, :]
    moves.append(pltpu.make_async_copy(out, near, sems.at[count]))
    moves[-1].start()
    for move in moves:
        move.wait()


def room(mebibytes):
    return pltpu.CompilerParams(vmem_limit_bytes=mebibytes << 20)


def shape(dims, kind):
    return jax.ShapeDtypeStruct(dims, kind)


def carried(summary, rows, backward):
    pairs = lax.axis_size("tm") // 2
    other = swap(summary, "tm", 1)
    whole = pl.pallas_call(
        functools.partial(pair_kernel, rows, backward, 1), out_shape=shape(summary.shape, f32), compiler_params=room(1)
    )(summary, other)
    return [other, whole] + [swap(whole, "tm", 2 * key) for key in range(1, pairs)]


def local(returns, innovations, decay_rate, innov_scale, loadings, noise_scale):
    factors, draws, steps = innovations.shape
    series = returns.shape[1]
    parts, spans = lax.axis_size("series"), lax.axis_size("tm")
    where, when = lax.axis_index("series"), lax.axis_index("tm")
    tiles = steps // LANES
    all_factors = factors * parts
    wide = all_factors * draws // LANES

    innov = innovations.reshape(factors, draws, tiles, LANES).transpose(0, 2, 1, 3)
    innov = innov.reshape(factors * tiles * draws, LANES)
    numbers = [where ^ key for key in range(parts)] + [1 - when % 2]
    numbers += [(when // 2) ^ key for key in range(spans // 2)]
    decay_rate, numbers = lax.optimization_barrier((decay_rate, numbers))
    seats, far_core = numbers[:parts], numbers[parts]
    chips_at = numbers[parts + 1:]
    spread, beyond, product, decays = pl.pallas_call(
        functools.partial(beyond_kernel, tiles),
        out_shape=(
            shape((factors, steps), f32),
            shape((factors, steps), f32),
            shape((1, factors), f32),
            shape((factors, steps), f32),
        ),
        name="beyond",
        cost_estimate=pl.CostEstimate(flops=2_000_000_000, bytes_accessed=1 << 20, transcendentals=0),
        compiler_params=room(2),
    )(decay_rate)
    pushes, summary, squares = pl.pallas_call(
        functools.partial(edge_kernel, draws, tiles),
        out_shape=(
            shape((draws, factors, steps), f32),
            shape((draws + 1, factors), f32),
            shape((draws, LANES), f32),
        ),
        name="edge",
        compiler_params=room(3),
    )(innov, innov_scale.reshape(1, factors), spread, beyond, product)
    local_paths, running = pl.pallas_call(
        functools.partial(forward_kernel, draws, tiles),
        out_shape=(shape((draws, factors, steps), f32), shape((factors, steps), f32)),
        name="forward_scan",
        compiler_params=room(4),
    )(decays, pushes)
    path_low = pl.pallas_call(
        functools.partial(enter_kernel, draws),
        out_shape=shape((draws, factors, steps), bf16),
        name="enter",
        compiler_params=room(2),
    )(local_paths, running, *carried(summary, draws + 1, False))

    pieces = [path_low] + [swap(path_low, "series", key) for key in range(1, parts)]
    noise = noise_scale.reshape(series // LANES, LANES)
    loads = loadings.transpose(1, 0, 2)
    loads_t = loadings.transpose(1, 2, 0)
    rows = min(512, series // 2)
    body = draws * tiles * factors
    still = lambda dims: pl.BlockSpec(dims, lambda i: (0,) * len(dims))
    size = series * wide
    half, piece = size // 2, size // spans
    grads, load_share = pl.pallas_call(
        functools.partial(residual_kernel, draws, parts),
        out_shape=(
            shape((parts, body + TAIL, LANES), f32),
            shape((2, half + TAIL, LANES), f32),
        ),
        grid_spec=pl.GridSpec(
            grid=(series // rows,),
            in_specs=[still((draws, factors, steps))] * parts
            + [
                pl.BlockSpec((steps, rows), lambda i: (0, i)),
                pl.BlockSpec((draws, rows, all_factors), lambda i: (0, i, 0)),
                pl.BlockSpec((draws, all_factors, rows), lambda i: (0, 0, i)),
                still((series // LANES, LANES)),
                still((draws, LANES)),
            ],
            out_specs=[
                still((parts, body + TAIL, LANES)),
                still((2, half + TAIL, LANES)),
            ],
            scratch_shapes=[
                pltpu.VMEM((draws, all_factors, steps), bf16),
                pltpu.VMEM((draws, LANES), f32),
                pltpu.VMEM((8, LANES), f32),
            ],
        ),
        name="residual",
        compiler_params=room(16),
    )(*pieces, returns, loads, loads_t, noise, squares)

    pick = lambda value, place: lax.dynamic_slice(value, (place, 0, 0), (1,) + value.shape[1:], allow_negative_indices=False)[0]
    sent = [pick(grads, place).astype(f16) for place in seats[1:]]
    arrived = [swap(value, "series", key) for key, value in enumerate(sent, 1)]

    chips = spans // 2
    whole = pl.BlockSpec(memory_space=pltpu.VMEM)
    distant = pl.BlockSpec(memory_space=pltpu.HBM)
    other = swap(pick(load_share, far_core).astype(f16), "tm", 1).astype(f32)
    kept = pl.pallas_call(
        join_kernel,
        out_shape=shape((chips, piece + TAIL, LANES), f32),
        in_specs=[whole, whole],
        out_specs=whole,
        name="join",
        compiler_params=room(8),
    )(load_share, other)
    others = [swap(pick(kept, chips_at[key]).astype(f16), "tm", 2 * key).astype(f32) for key in range(1, chips)]
    total, factor = pl.pallas_call(
        functools.partial(total_kernel, float(math.ceil(math.log2(chips)))),
        out_shape=(shape((piece, LANES), f32), shape((1, LANES), f32)),
        in_specs=[whole] * chips,
        out_specs=(whole, whole),
        name="total",
        compiler_params=room(4),
    )(kept, *others)
    total = lax.optimization_barrier(total.astype(f16))
    totals = [total] + [swap(total, "tm", 2 * key) for key in range(1, chips)]
    passed = [swap(value, "tm", 1) for value in totals]
    path_grads, leaving = pl.pallas_call(
        functools.partial(gather_kernel, draws, tiles, parts),
        out_shape=(shape((body, LANES), f32), shape((2 * draws + 1, factors), f32)),
        name="gather",
        compiler_params=room(4),
    )(running, summary, grads, *[value.astype(f32) for value in arrived])
    levels = LANES.bit_length() - 1
    flat = shape((factors, steps), f32)
    gates, inner, weight, fade = pl.pallas_call(
        functools.partial(unwind_kernel, tiles),
        out_shape=(shape((levels, factors, steps), f32), flat, flat, flat),
        name="unwind",
        compiler_params=room(4),
    )(decays, innov_scale.reshape(1, factors))
    local_adjoint = pl.pallas_call(
        functools.partial(backward_kernel, draws, tiles),
        out_shape=shape((draws, factors, steps), f32),
        name="backward_scan",
        compiler_params=room(4),
    )(gates, inner, path_grads)
    climb = carried(leaving, draws + 1, True)
    grad_innov, log_density, grad_load = pl.pallas_call(
        functools.partial(leave_kernel, draws, tiles, float(spans * parts), 2 * chips),
        out_shape=(shape(innov.shape, f32), shape((draws,), f32), shape((size, LANES), f32)),
        in_specs=[whole] * (2 * chips + 4 + len(climb)),
        out_specs=(distant, pl.BlockSpec(memory_space=pltpu.SMEM), distant),
        scratch_shapes=[pltpu.VMEM(innov.shape, f32), pltpu.SemaphoreType.DMA((2 * chips + 1,))],
        name="leave",
        compiler_params=room(6),
    )(*[value.astype(f32) * factor for value in totals + passed], local_adjoint, fade, weight, innov, *climb)
    grad_load = grad_load.reshape(series, all_factors // LANES, draws, LANES).transpose(0, 2, 1, 3)
    grad_load = grad_load.reshape(series, draws, all_factors)
    grad_innov = grad_innov.reshape(factors, tiles, draws, LANES).transpose(0, 2, 1, 3)
    grad_innov = grad_innov.reshape(factors, draws, steps)

    return (grad_innov, grad_load, log_density)


def solution(mesh):
    placed = (
        P("tm", "series"),
        P("series", None, "tm"),
        P("series", "tm"),
        P("series"),
        P("series", None, None),
        P("series"),
    )

    return jax.shard_map(
        local,
        mesh=mesh,
        in_specs=placed,
        out_specs=(P("series", None, "tm"), P("series", None, None), P()),
        check_vma=False,
    )
```

```python
import functools
import math

import jax
import jax.numpy as jnp
from jax import lax
from jax.experimental import pallas as pl
from jax.experimental.pallas import tpu as pltpu
from jax.sharding import PartitionSpec as P


freedom = 5.0
LANES = 128
TAIL = 16
f32 = jnp.float32
bf16 = jnp.bfloat16
f16 = jnp.float16


def swap(value, axis, key):
    count = lax.axis_size(axis)
    return lax.ppermute(value, axis, [(i, i ^ key) for i in range(count)])


def eye(size):
    rows = lax.broadcasted_iota(jnp.int32, (size, size), 0)
    return rows == lax.broadcasted_iota(jnp.int32, (size, size), 1)


def to_column(row, same):
    return jnp.sum(jnp.where(same, row, 0.0), axis=1, keepdims=True)


def to_row(column, same):
    return jnp.sum(jnp.where(same, column, 0.0), axis=0, keepdims=True)


def tile_scan(decay, pushes, backward):
    lane = lax.broadcasted_iota(jnp.int32, decay.shape, 1)
    width = decay.shape[1]
    step = 1
    while step < width:
        turn = width - step if backward else step
        inside = lane < width - step if backward else lane >= step
        gate = jnp.where(inside, decay, 0.0)
        pushes = [p + gate * pltpu.roll(p, turn, 1) for p in pushes]
        decay = decay * jnp.where(inside, pltpu.roll(decay, turn, 1), 1.0)
        step *= 2
    return decay, pushes


def block_scan(decays, pushes, backward):
    tiles = len(decays)
    draws = len(pushes[0])
    order = range(tiles - 1, -1, -1) if backward else range(tiles)
    edge = slice(0, 1) if backward else slice(LANES - 1, LANES)
    run, out = [None] * tiles, [None] * tiles
    carry = None
    for j in order:
        a, b = tile_scan(decays[j], pushes[j], backward)
        if carry is not None:
            b = [b[d] + a * carry[1][d] for d in range(draws)]
            a = a * carry[0]
        run[j], out[j] = a, b
        carry = (a[:, edge], [x[:, edge] for x in b])
    return run, out, carry


def beyond_kernel(tiles, decay, spread, beyond, product, held):
    factors = decay.shape[0]
    held[...] = decay[...]
    lane = lax.broadcasted_iota(jnp.int32, (factors, LANES), 1)
    after = jnp.ones((factors, 1), f32)
    for j in range(tiles - 1, -1, -1):
        part = slice(j * LANES, (j + 1) * LANES)
        a = decay[:, part]
        spread[:, part] = jnp.sqrt((1.0 - a) * (1.0 + a))
        run, _ = tile_scan(a, [], True)
        beyond[:, part] = jnp.where(lane < LANES - 1, pltpu.roll(run, LANES - 1, 1), 1.0) * after
        after = after * run[:, 0:1]
    product[...] = to_row(after, eye(factors))


def edge_kernel(draws, tiles, innov, scale, spread, beyond, product, pushes, summary, squares):
    factors = spread.shape[0]
    same = eye(factors)
    column = to_column(scale[...], same)
    total = [jnp.zeros((factors, LANES), f32)] * draws
    ends = [jnp.zeros((factors, LANES), f32)] * draws
    for j in range(tiles):
        part = slice(j * LANES, (j + 1) * LANES)
        w = spread[:, part] * column
        for d in range(draws):
            x = innov[pl.ds(j * draws + d, factors, stride=tiles * draws), :]
            push = w * x
            pushes[d, :, part] = push
            total[d] = total[d] + x * x
            ends[d] = ends[d] + push * beyond[:, part]
    summary[0:1, :] = product[...]
    for d in range(draws):
        summary[d + 1:d + 2, :] = to_row(jnp.sum(ends[d], axis=1, keepdims=True), same)
        squares[d:d + 1, :] = jnp.sum(total[d], axis=0, keepdims=True)


def forward_kernel(draws, tiles, decay, pushed, local, running):
    parts = [slice(j * LANES, (j + 1) * LANES) for j in range(tiles)]
    decays = [decay[:, part] for part in parts]
    pushes = [[pushed[d, :, part] for d in range(draws)] for part in parts]
    run, out, _ = block_scan(decays, pushes, False)
    for j in range(tiles):
        running[:, j * LANES:(j + 1) * LANES] = run[j]
        for d in range(draws):
            local[d, :, j * LANES:(j + 1) * LANES] = out[j][d]


def seat(backward):
    count, mine = lax.axis_size("tm"), lax.axis_index("tm")
    return count - 1 - mine if backward else mine


def pair_kernel(rows, backward, bit, summary, other, whole):
    later = (seat(backward) // bit) % 2 == 1
    mine, theirs = summary[...], other[...]
    first, second = jnp.where(later, theirs, mine), jnp.where(later, mine, theirs)
    whole[0:1, :] = first[0:1] * second[0:1]
    whole[1:rows, :] = second[0:1] * first[1:rows] + second[1:rows]
    if rows < mine.shape[0]:
        whole[rows:, :] = first[rows:] + second[rows:]


def entered(rows, backward, other, totals):
    mine = seat(backward)
    later, pair, pairs = mine % 2 == 1, mine // 2, len(totals)
    theirs = other[...]
    values = [total[...] for total in totals]
    entering = jnp.zeros_like(theirs[1:rows])
    summed = jnp.zeros_like(theirs[rows:]) if rows < theirs.shape[0] else None
    for place in range(pairs):
        here = values[0]
        for key in range(1, pairs):
            here = jnp.where((pair ^ key) == place, values[key], here)
        entering = jnp.where(place < pair, here[0:1] * entering + here[1:rows], entering)
        if summed is not None:
            summed = summed + here[rows:]
    return jnp.where(later, theirs[0:1] * entering + theirs[1:rows], entering), summed


def enter_kernel(draws, local, running, other, *refs):
    totals, path = refs[:-1], refs[-1]
    same = eye(running.shape[0])
    entering, _ = entered(draws + 1, False, other, totals)
    for d in range(draws):
        column = to_column(entering[d:d + 1, :], same)
        path[d] = (local[d] + running[...] * column).astype(bf16)


def when(condition):
    return (lambda body: body()) if condition is True else pl.when(condition)


def residual_kernel(draws, parts, count, *refs):
    pieces, (returns, loads, loads_t, noise, squares, grads, shares, paths, density, top) = refs[:parts], refs[parts:]
    factors = pieces[0].shape[1]
    step = 0 if count == 1 else pl.program_id(0)
    wide = paths.shape[1] // LANES
    share_rows = returns.shape[1] // 2 if count == 1 else returns.shape[1]
    side = step // max(count // 2, 1)
    base = (step % max(count // 2, 1)) * (share_rows * wide * draws)

    @when(step == 0)
    def _():
        for n in range(parts):
            start = pl.multiple_of((lax.axis_index("series") ^ n) * factors, factors)
            paths[:, pl.ds(start, factors), :] = pieces[n][...]
        if count > 1:
            grads[...] = jnp.zeros_like(grads)
        density[...] = jnp.zeros_like(density)
        top[...] = jnp.zeros_like(top)

    seen = returns[...].T.astype(f32)
    rows = seen.shape[0]
    same = eye(LANES)
    groups = rows // LANES
    spread = [to_column(noise[pl.ds(step * groups + g, 1), :], same) for g in range(groups)]
    spread = jnp.concatenate(spread, axis=0)
    s2 = freedom * (spread * spread)
    inverse = 1.0 / s2
    tiles = seen.shape[1] // LANES
    half = rows // 2
    for d in range(draws):
        fitted = jnp.dot(loads[d], paths[d], preferred_element_type=f32)
        residual = seen - fitted
        square = residual * residual
        pulled = ((freedom + 1.0) * residual / (s2 + square)).astype(bf16)
        ratio = square * inverse
        first, second = ratio[:half], ratio[half:]
        both = jnp.log1p(first + second * (1.0 + first))
        both = jnp.sum(both, axis=0, keepdims=True)
        lanes = both[:, :LANES]
        for j in range(1, both.shape[1] // LANES):
            lanes = lanes + both[:, j * LANES:(j + 1) * LANES]
        density[d:d + 1, :] += lanes
        product = jnp.dot(loads_t[d], pulled, preferred_element_type=f32)
        for n in range(parts):
            for j in range(tiles):
                to = slice((d * tiles + j) * factors, (d * tiles + j + 1) * factors)
                part = product[n * factors:(n + 1) * factors, j * LANES:(j + 1) * LANES]
                grads[n, to, :] = part if count == 1 else grads[n, to, :] + part
        share = lax.dot_general(pulled, paths[d], (((1,), (1,)), ((), ())), preferred_element_type=f32)
        most = top[...]
        for j in range(wide):
            tile = share[:, j * LANES:(j + 1) * LANES]
            for part in range(rows // share_rows):
                piece = tile[part * share_rows:(part + 1) * share_rows]
                shares[side + part, pl.ds(base + (j * draws + d), share_rows, stride=wide * draws), :] = piece
            most = jnp.maximum(most, jnp.max(jnp.abs(tile).reshape(rows // 8, 8, LANES), axis=0))
        top[...] = most

    @when(step == count - 1)
    def _():
        body = draws * tiles * factors
        cells = count * rows * seen.shape[1]
        peak = jnp.zeros((1, LANES), f32)
        for n in range(parts):
            peak = jnp.maximum(peak, jnp.max(jnp.abs(grads[n, :body, :]), axis=0, keepdims=True))
        level = exponent(peak)
        tail = [level]
        for d in range(draws):
            value = -(freedom + 1.0) * 0.5 * density[d:d + 1, :] - 0.5 * squares[d:d + 1, :]
            tail += coded(jnp.sum(value, axis=1, keepdims=True) * (1.0 / cells))
        tail = stacked(tail)
        factor = jnp.exp2(15.0 - level)
        for n in range(parts):
            grads[n, :body, :] = grads[n, :body, :] * factor
            grads[n, body:, :] = tail
        half = shares.shape[1] - TAIL
        level = exponent(jnp.max(top[...], axis=0, keepdims=True))
        factor = jnp.exp2(15.0 - level)
        for n in range(2):
            shares[n, :half, :] = shares[n, :half, :] * factor
            shares[n, half:, :] = stacked([level])


def coded(value):
    value = jnp.broadcast_to(value, (1, LANES))
    level = exponent(jnp.abs(value))
    left = value * jnp.exp2(-level)
    codes = [level]
    unit = 1024.0
    for _ in range(3):
        code = (left * unit + 12582912.0) - 12582912.0
        codes.append(code)
        left = left - code * (1.0 / unit)
        unit = unit * 1024.0
    return codes


def decoded(rows):
    level, first, second, third = [rows[n:n + 1, :] for n in range(4)]
    small = 1.0 / 1024.0
    return jnp.exp2(level) * (first + (second + third * small) * small) * small


def stacked(rows):
    place = lax.broadcasted_iota(jnp.int32, (TAIL, LANES), 0)
    out = jnp.zeros((TAIL, LANES), f32)
    for n, row in enumerate(rows):
        out = jnp.where(place == n, row, out)
    return out


def exponent(lanes):
    top = jnp.maximum(jnp.max(lanes, axis=1, keepdims=True), 1e-30)
    return jnp.broadcast_to(jnp.ceil(jnp.log(top) * (1.0 / math.log(2.0))), lanes.shape)


def join_kernel(mine, other, out):
    core = lax.axis_index("tm") % 2
    body = other.shape[0] - TAIL
    chips = out.shape[0]
    piece = body // chips
    own, far = mine[core, body:body + 1, :], other[body:body + 1, :]
    level = jnp.maximum(own, far) + 1.0
    own, far = jnp.exp2(own - level), jnp.exp2(far - level)
    for n in range(chips):
        rows = slice(n * piece, (n + 1) * piece)
        out[n, :piece, :] = mine[core, rows, :] * own + other[rows, :] * far
        out[n, piece:, :] = stacked([level])


def total_kernel(lift, mine, *refs):
    others, (out, factor) = refs[:-2], refs[-2:]
    piece = out.shape[0]
    here = lax.axis_index("tm") // 2
    levels = [mine[here, piece:piece + 1, :]] + [other[piece:piece + 1, :] for other in others]
    top = levels[0]
    for level in levels[1:]:
        top = jnp.maximum(top, level)
    top = top + lift
    total = mine[here, :piece, :] * jnp.exp2(levels[0] - top)
    for level, other in zip(levels[1:], others):
        total = total + other[:piece, :] * jnp.exp2(level - top)
    out[...] = total
    factor[...] = jnp.exp2(top - 15.0)


def gather_kernel(draws, tiles, parts, running, products, mine, *refs):
    others, (gathered, summary) = refs[:-2], refs[-2:]
    factors = running.shape[0]
    body = draws * tiles * factors
    here = lax.axis_index("series")
    tails = [mine[here, body:, :]] + [other[body:, :] for other in others]
    scales = [jnp.exp2(rows[0:1, :] - 15.0) for rows in tails]
    same = eye(factors)
    summary[0:1, :] = products[0:1, :]
    for d in range(draws):
        known = [decoded(rows[1 + 4 * d:5 + 4 * d, :]) for rows in tails]
        density = jnp.zeros((1, LANES), f32)
        for place in range(parts):
            for n in range(parts):
                density = density + jnp.where((here ^ n) == place, known[n], 0.0)
        summary[draws + 1 + d:draws + 2 + d, :] = density[:, :factors]
        leaving = jnp.zeros((factors, LANES), f32)
        for j in range(tiles):
            rows = slice((d * tiles + j) * factors, (d * tiles + j + 1) * factors)
            value = mine[here, rows, :] * scales[0]
            for other, scale in zip(others, scales[1:]):
                value = value + other[rows, :] * scale
            gathered[rows, :] = value
            leaving = leaving + value * running[:, j * LANES:(j + 1) * LANES]
        summary[d + 1:d + 2, :] = to_row(jnp.sum(leaving, axis=1, keepdims=True), same)


def unwind_kernel(tiles, decay, scale, gates, inner, weight, fade):
    factors = decay.shape[0]
    lane = lax.broadcasted_iota(jnp.int32, (factors, LANES), 1)
    sized = to_column(scale[...], eye(factors))
    beyond = jnp.ones((factors, 1), f32)
    for j in range(tiles - 1, -1, -1):
        part = slice(j * LANES, (j + 1) * LANES)
        a = decay[:, part]
        w = jnp.sqrt((1.0 - a) * (1.0 + a)) * sized
        weight[:, part] = w
        if j + 1 < tiles:
            after = decay[:, (j + 1) * LANES:(j + 2) * LANES][:, 0:1]
        else:
            after = jnp.ones((factors, 1), f32)
        run = jnp.where(lane < LANES - 1, pltpu.roll(a, LANES - 1, 1), after)
        for level in range(gates.shape[0]):
            step = 1 << level
            inside = lane < LANES - step
            gates[level, :, part] = jnp.where(inside, run, 0.0)
            run = run * jnp.where(inside, pltpu.roll(run, LANES - step, 1), 1.0)
        inner[:, part] = run
        fade[:, part] = w * run * beyond
        beyond = beyond * run[:, 0:1]


def backward_kernel(draws, tiles, gates, inner, grads, local):
    factors = inner.shape[0]
    carry = None
    for j in range(tiles - 1, -1, -1):
        part = slice(j * LANES, (j + 1) * LANES)
        rows = lambda d: slice((d * tiles + j) * factors, (d * tiles + j + 1) * factors)
        values = [grads[rows(d), :] for d in range(draws)]
        for level in range(gates.shape[0]):
            gate = gates[level, :, part]
            values = [p + gate * pltpu.roll(p, LANES - (1 << level), 1) for p in values]
        if carry is not None:
            values = [values[d] + inner[:, part] * carry[d] for d in range(draws)]
        for d in range(draws):
            local[d, :, part] = values[d]
        carry = [p[:, 0:1] for p in values]


def leave_kernel(draws, tiles, cells, count, *refs):
    pieces, refs = refs[:count], refs[count:]
    (local, fade, weight, innov), climb, (near, density, far, out, sems) = refs[:4], refs[4:-5], refs[-5:]
    lines, chips = pieces[0].shape[0], count // 2
    mine = lax.axis_index("tm")
    moves = []
    for n, piece in enumerate(pieces):
        side = (mine + n // chips) % 2
        start = pl.multiple_of((side * chips + ((mine // 2) ^ (n % chips))) * lines, lines)
        moves.append(pltpu.make_async_copy(piece, far.at[pl.ds(start, lines), :], sems.at[n]))
    for move in moves:
        move.start()
    factors = fade.shape[0]
    same = eye(factors)
    arriving, summed = entered(draws + 1, True, climb[0], climb[1:])
    columns = [to_column(arriving[d:d + 1, :], same) for d in range(draws)]
    for d in range(draws):
        density[d] = jnp.max(summed[d:d + 1, :]) * (1.0 / cells)
    for j in range(tiles):
        part = slice(j * LANES, (j + 1) * LANES)
        for d in range(draws):
            rows = pl.ds(j * draws + d, factors, stride=tiles * draws)
            out[rows, :] = weight[:, part] * local[d, :, part] + fade[:, part] * columns[d] - innov[rows, :]
    moves.append(pltpu.make_async_copy(out, near, sems.at[count]))
    moves[-1].start()
    for move in moves:
        move.wait()


def room(mebibytes):
    return pltpu.CompilerParams(vmem_limit_bytes=mebibytes << 20)


def shape(dims, kind):
    return jax.ShapeDtypeStruct(dims, kind)


def carried(summary, rows, backward):
    pairs = lax.axis_size("tm") // 2
    other = swap(summary, "tm", 1)
    whole = pl.pallas_call(
        functools.partial(pair_kernel, rows, backward, 1), out_shape=shape(summary.shape, f32), compiler_params=room(1)
    )(summary, other)
    return [other, whole] + [swap(whole, "tm", 2 * key) for key in range(1, pairs)]


def local(returns, innovations, decay_rate, innov_scale, loadings, noise_scale):
    factors, draws, steps = innovations.shape
    series = returns.shape[1]
    parts, spans = lax.axis_size("series"), lax.axis_size("tm")
    where, when = lax.axis_index("series"), lax.axis_index("tm")
    tiles = steps // LANES
    all_factors = factors * parts
    wide = all_factors * draws // LANES

    innov = innovations.reshape(factors, draws, tiles, LANES).transpose(0, 2, 1, 3)
    innov = innov.reshape(factors * tiles * draws, LANES)
    numbers = [where ^ key for key in range(parts)] + [1 - when % 2]
    numbers += [(when // 2) ^ key for key in range(spans // 2)]
    decay_rate, numbers = lax.optimization_barrier((decay_rate, numbers))
    seats, far_core = numbers[:parts], numbers[parts]
    chips_at = numbers[parts + 1:]
    spread, beyond, product, decays = pl.pallas_call(
        functools.partial(beyond_kernel, tiles),
        out_shape=(
            shape((factors, steps), f32),
            shape((factors, steps), f32),
            shape((1, factors), f32),
            shape((factors, steps), f32),
        ),
        name="beyond",
        cost_estimate=pl.CostEstimate(flops=2_000_000_000, bytes_accessed=1 << 20, transcendentals=0),
        compiler_params=room(2),
    )(decay_rate)
    pushes, summary, squares = pl.pallas_call(
        functools.partial(edge_kernel, draws, tiles),
        out_shape=(
            shape((draws, factors, steps), f32),
            shape((draws + 1, factors), f32),
            shape((draws, LANES), f32),
        ),
        name="edge",
        compiler_params=room(3),
    )(innov, innov_scale.reshape(1, factors), spread, beyond, product)
    local_paths, running = pl.pallas_call(
        functools.partial(forward_kernel, draws, tiles),
        out_shape=(shape((draws, factors, steps), f32), shape((factors, steps), f32)),
        name="forward_scan",
        compiler_params=room(4),
    )(decays, pushes)
    path_low = pl.pallas_call(
        functools.partial(enter_kernel, draws),
        out_shape=shape((draws, factors, steps), bf16),
        name="enter",
        compiler_params=room(2),
    )(local_paths, running, *carried(summary, draws + 1, False))

    pieces = [path_low] + [swap(path_low, "series", key) for key in range(1, parts)]
    noise = noise_scale.reshape(series // LANES, LANES)
    loads = loadings.transpose(1, 0, 2)
    loads_t = loadings.transpose(1, 2, 0)
    rows = min(1024, series)
    body = draws * tiles * factors
    still = lambda dims: pl.BlockSpec(dims, lambda i: (0,) * len(dims))
    size = series * wide
    half, piece = size // 2, size // spans
    grads, load_share = pl.pallas_call(
        functools.partial(residual_kernel, draws, parts, series // rows),
        out_shape=(
            shape((parts, body + TAIL, LANES), f32),
            shape((2, half + TAIL, LANES), f32),
        ),
        grid_spec=pl.GridSpec(
            grid=() if rows == series else (series // rows,),
            in_specs=[pl.BlockSpec(memory_space=pltpu.VMEM)] * (parts + 5) if rows == series else [still((draws, factors, steps))] * parts
            + [
                pl.BlockSpec((steps, rows), lambda i: (0, i)),
                pl.BlockSpec((draws, rows, all_factors), lambda i: (0, i, 0)),
                pl.BlockSpec((draws, all_factors, rows), lambda i: (0, 0, i)),
                still((series // LANES, LANES)),
                still((draws, LANES)),
            ],
            out_specs=[pl.BlockSpec(memory_space=pltpu.VMEM)] * 2 if rows == series else [
                still((parts, body + TAIL, LANES)),
                still((2, half + TAIL, LANES)),
            ],
            scratch_shapes=[
                pltpu.VMEM((draws, all_factors, steps), bf16),
                pltpu.VMEM((draws, LANES), f32),
                pltpu.VMEM((8, LANES), f32),
            ],
        ),
        name="residual",
        compiler_params=room(28),
    )(*pieces, returns, loads, loads_t, noise, squares)

    pick = lambda value, place: lax.dynamic_slice(value, (place, 0, 0), (1,) + value.shape[1:], allow_negative_indices=False)[0]
    sent = [pick(grads, place).astype(f16) for place in seats[1:]]
    arrived = [swap(value, "series", key) for key, value in enumerate(sent, 1)]

    chips = spans // 2
    whole = pl.BlockSpec(memory_space=pltpu.VMEM)
    distant = pl.BlockSpec(memory_space=pltpu.HBM)
    other = swap(pick(load_share, far_core).astype(f16), "tm", 1).astype(f32)
    kept = pl.pallas_call(
        join_kernel,
        out_shape=shape((chips, piece + TAIL, LANES), f32),
        in_specs=[whole, whole],
        out_specs=whole,
        name="join",
        compiler_params=room(8),
    )(load_share, other)
    others = [swap(pick(kept, chips_at[key]).astype(f16), "tm", 2 * key).astype(f32) for key in range(1, chips)]
    total, factor = pl.pallas_call(
        functools.partial(total_kernel, float(math.ceil(math.log2(chips)))),
        out_shape=(shape((piece, LANES), f32), shape((1, LANES), f32)),
        in_specs=[whole] * chips,
        out_specs=(whole, whole),
        name="total",
        compiler_params=room(4),
    )(kept, *others)
    total = lax.optimization_barrier(total.astype(f16))
    totals = [total] + [swap(total, "tm", 2 * key) for key in range(1, chips)]
    passed = [swap(value, "tm", 1) for value in totals]
    path_grads, leaving = pl.pallas_call(
        functools.partial(gather_kernel, draws, tiles, parts),
        out_shape=(shape((body, LANES), f32), shape((2 * draws + 1, factors), f32)),
        name="gather",
        compiler_params=room(4),
    )(running, summary, grads, *[value.astype(f32) for value in arrived])
    levels = LANES.bit_length() - 1
    flat = shape((factors, steps), f32)
    gates, inner, weight, fade = pl.pallas_call(
        functools.partial(unwind_kernel, tiles),
        out_shape=(shape((levels, factors, steps), f32), flat, flat, flat),
        name="unwind",
        compiler_params=room(4),
    )(decays, innov_scale.reshape(1, factors))
    local_adjoint = pl.pallas_call(
        functools.partial(backward_kernel, draws, tiles),
        out_shape=shape((draws, factors, steps), f32),
        name="backward_scan",
        compiler_params=room(4),
    )(gates, inner, path_grads)
    climb = carried(leaving, draws + 1, True)
    grad_innov, log_density, grad_load = pl.pallas_call(
        functools.partial(leave_kernel, draws, tiles, float(spans * parts), 2 * chips),
        out_shape=(shape(innov.shape, f32), shape((draws,), f32), shape((size, LANES), f32)),
        in_specs=[whole] * (2 * chips + 4 + len(climb)),
        out_specs=(distant, pl.BlockSpec(memory_space=pltpu.SMEM), distant),
        scratch_shapes=[pltpu.VMEM(innov.shape, f32), pltpu.SemaphoreType.DMA((2 * chips + 1,))],
        name="leave",
        compiler_params=room(6),
    )(*[value.astype(f32) * factor for value in totals + passed], local_adjoint, fade, weight, innov, *climb)
    grad_load = grad_load.reshape(series, all_factors // LANES, draws, LANES).transpose(0, 2, 1, 3)
    grad_load = grad_load.reshape(series, draws, all_factors)
    grad_innov = grad_innov.reshape(factors, tiles, draws, LANES).transpose(0, 2, 1, 3)
    grad_innov = grad_innov.reshape(factors, draws, steps)

    return (grad_innov, grad_load, log_density)


def solution(mesh):
    placed = (
        P("tm", "series"),
        P("series", None, "tm"),
        P("series", "tm"),
        P("series"),
        P("series", None, None),
        P("series"),
    )

    return jax.shard_map(
        local,
        mesh=mesh,
        in_specs=placed,
        out_specs=(P("series", None, "tm"), P("series", None, None), P()),
        check_vma=False,
    )
```

```python
import functools
import math

import jax
import jax.numpy as jnp
from jax import lax
from jax.experimental import pallas as pl
from jax.experimental.pallas import tpu as pltpu
from jax.sharding import PartitionSpec as P


freedom = 5.0
LANES = 128
TAIL = 16
f32 = jnp.float32
bf16 = jnp.bfloat16
f16 = jnp.float16


def swap(value, axis, key):
    count = lax.axis_size(axis)
    return lax.ppermute(value, axis, [(i, i ^ key) for i in range(count)])


def eye(size):
    rows = lax.broadcasted_iota(jnp.int32, (size, size), 0)
    return rows == lax.broadcasted_iota(jnp.int32, (size, size), 1)


def to_column(row, same):
    return jnp.sum(jnp.where(same, row, 0.0), axis=1, keepdims=True)


def to_row(column, same):
    return jnp.sum(jnp.where(same, column, 0.0), axis=0, keepdims=True)


def tile_scan(decay, pushes, backward):
    lane = lax.broadcasted_iota(jnp.int32, decay.shape, 1)
    width = decay.shape[1]
    step = 1
    while step < width:
        turn = width - step if backward else step
        inside = lane < width - step if backward else lane >= step
        gate = jnp.where(inside, decay, 0.0)
        pushes = [p + gate * pltpu.roll(p, turn, 1) for p in pushes]
        decay = decay * jnp.where(inside, pltpu.roll(decay, turn, 1), 1.0)
        step *= 2
    return decay, pushes


def block_scan(decays, pushes, backward):
    tiles = len(decays)
    draws = len(pushes[0])
    order = range(tiles - 1, -1, -1) if backward else range(tiles)
    edge = slice(0, 1) if backward else slice(LANES - 1, LANES)
    run, out = [None] * tiles, [None] * tiles
    carry = None
    for j in order:
        a, b = tile_scan(decays[j], pushes[j], backward)
        if carry is not None:
            b = [b[d] + a * carry[1][d] for d in range(draws)]
            a = a * carry[0]
        run[j], out[j] = a, b
        carry = (a[:, edge], [x[:, edge] for x in b])
    return run, out, carry


def beyond_kernel(tiles, decay, spread, beyond, product, held):
    factors = decay.shape[0]
    held[...] = decay[...]
    lane = lax.broadcasted_iota(jnp.int32, (factors, LANES), 1)
    after = jnp.ones((factors, 1), f32)
    for j in range(tiles - 1, -1, -1):
        part = slice(j * LANES, (j + 1) * LANES)
        a = decay[:, part]
        spread[:, part] = jnp.sqrt((1.0 - a) * (1.0 + a))
        run, _ = tile_scan(a, [], True)
        beyond[:, part] = jnp.where(lane < LANES - 1, pltpu.roll(run, LANES - 1, 1), 1.0) * after
        after = after * run[:, 0:1]
    product[...] = to_row(after, eye(factors))


def edge_kernel(draws, tiles, innov, scale, spread, beyond, product, pushes, summary, squares):
    factors = spread.shape[0]
    same = eye(factors)
    column = to_column(scale[...], same)
    total = [jnp.zeros((factors, LANES), f32)] * draws
    ends = [jnp.zeros((factors, LANES), f32)] * draws
    for j in range(tiles):
        part = slice(j * LANES, (j + 1) * LANES)
        w = spread[:, part] * column
        for d in range(draws):
            x = innov[pl.ds(j * draws + d, factors, stride=tiles * draws), :]
            push = w * x
            pushes[d, :, part] = push
            total[d] = total[d] + x * x
            ends[d] = ends[d] + push * beyond[:, part]
    summary[0:1, :] = product[...]
    for d in range(draws):
        summary[d + 1:d + 2, :] = to_row(jnp.sum(ends[d], axis=1, keepdims=True), same)
        squares[d:d + 1, :] = jnp.sum(total[d], axis=0, keepdims=True)


def forward_kernel(draws, tiles, decay, pushed, local, running):
    parts = [slice(j * LANES, (j + 1) * LANES) for j in range(tiles)]
    decays = [decay[:, part] for part in parts]
    pushes = [[pushed[d, :, part] for d in range(draws)] for part in parts]
    run, out, _ = block_scan(decays, pushes, False)
    for j in range(tiles):
        running[:, j * LANES:(j + 1) * LANES] = run[j]
        for d in range(draws):
            local[d, :, j * LANES:(j + 1) * LANES] = out[j][d]


def seat(backward):
    count, mine = lax.axis_size("tm"), lax.axis_index("tm")
    return count - 1 - mine if backward else mine


def pair_kernel(rows, backward, bit, summary, other, whole):
    later = (seat(backward) // bit) % 2 == 1
    mine, theirs = summary[...], other[...]
    first, second = jnp.where(later, theirs, mine), jnp.where(later, mine, theirs)
    whole[0:1, :] = first[0:1] * second[0:1]
    whole[1:rows, :] = second[0:1] * first[1:rows] + second[1:rows]
    if rows < mine.shape[0]:
        whole[rows:, :] = first[rows:] + second[rows:]


def entered(rows, backward, other, totals):
    mine = seat(backward)
    later, pair, pairs = mine % 2 == 1, mine // 2, len(totals)
    theirs = other[...]
    values = [total[...] for total in totals]
    entering = jnp.zeros_like(theirs[1:rows])
    summed = jnp.zeros_like(theirs[rows:]) if rows < theirs.shape[0] else None
    for place in range(pairs):
        here = values[0]
        for key in range(1, pairs):
            here = jnp.where((pair ^ key) == place, values[key], here)
        entering = jnp.where(place < pair, here[0:1] * entering + here[1:rows], entering)
        if summed is not None:
            summed = summed + here[rows:]
    return jnp.where(later, theirs[0:1] * entering + theirs[1:rows], entering), summed


def enter_kernel(draws, local, running, other, *refs):
    totals, path = refs[:-1], refs[-1]
    same = eye(running.shape[0])
    entering, _ = entered(draws + 1, False, other, totals)
    for d in range(draws):
        column = to_column(entering[d:d + 1, :], same)
        path[d] = (local[d] + running[...] * column).astype(bf16)


def when(condition):
    return (lambda body: body()) if condition is True else pl.when(condition)


def residual_kernel(draws, parts, count, *refs):
    pieces, (returns, loads, loads_t, noise, squares, grads, shares, paths, density, top) = refs[:parts], refs[parts:]
    factors = pieces[0].shape[1]
    step = 0 if count == 1 else pl.program_id(0)
    wide = paths.shape[1] // LANES
    share_rows = returns.shape[1] // 2 if count == 1 else returns.shape[1]
    side = step // max(count // 2, 1)
    base = (step % max(count // 2, 1)) * (share_rows * wide * draws)

    @when(step == 0)
    def _():
        for n in range(parts):
            start = pl.multiple_of((lax.axis_index("series") ^ n) * factors, factors)
            paths[:, pl.ds(start, factors), :] = pieces[n][...]
        if count > 1:
            grads[...] = jnp.zeros_like(grads)
        density[...] = jnp.zeros_like(density)
        top[...] = jnp.zeros_like(top)

    seen = returns[...].T.astype(f32)
    rows = seen.shape[0]
    same = eye(LANES)
    groups = rows // LANES
    spread = [to_column(noise[pl.ds(step * groups + g, 1), :], same) for g in range(groups)]
    spread = jnp.concatenate(spread, axis=0)
    s2 = freedom * (spread * spread)
    inverse = 1.0 / s2
    tiles = seen.shape[1] // LANES
    half = rows // 2
    for d in range(draws):
        fitted = jnp.dot(loads[d], paths[d], preferred_element_type=f32)
        residual = seen - fitted
        square = residual * residual
        pulled = ((freedom + 1.0) * residual / (s2 + square)).astype(bf16)
        ratio = square * inverse
        first, second = ratio[:half], ratio[half:]
        both = jnp.log1p(first + second * (1.0 + first))
        both = jnp.sum(both, axis=0, keepdims=True)
        lanes = both[:, :LANES]
        for j in range(1, both.shape[1] // LANES):
            lanes = lanes + both[:, j * LANES:(j + 1) * LANES]
        density[d:d + 1, :] += lanes
        product = jnp.dot(loads_t[d], pulled, preferred_element_type=f32)
        for n in range(parts):
            for j in range(tiles):
                to = slice((d * tiles + j) * factors, (d * tiles + j + 1) * factors)
                part = product[n * factors:(n + 1) * factors, j * LANES:(j + 1) * LANES]
                grads[n, to, :] = part if count == 1 else grads[n, to, :] + part
        share = lax.dot_general(pulled, paths[d], (((1,), (1,)), ((), ())), preferred_element_type=f32)
        most = top[...]
        for j in range(wide):
            tile = share[:, j * LANES:(j + 1) * LANES]
            for part in range(rows // share_rows):
                piece = tile[part * share_rows:(part + 1) * share_rows]
                shares[side + part, pl.ds(base + (j * draws + d), share_rows, stride=wide * draws), :] = piece
            most = jnp.maximum(most, jnp.max(jnp.abs(tile).reshape(rows // 8, 8, LANES), axis=0))
        top[...] = most

    @when(step == count - 1)
    def _():
        body = draws * tiles * factors
        cells = count * rows * seen.shape[1]
        peak = jnp.zeros((1, LANES), f32)
        for n in range(parts):
            peak = jnp.maximum(peak, jnp.max(jnp.abs(grads[n, :body, :]), axis=0, keepdims=True))
        level = exponent(peak)
        tail = [level]
        for d in range(draws):
            value = -(freedom + 1.0) * 0.5 * density[d:d + 1, :] - 0.5 * squares[d:d + 1, :]
            tail += coded(jnp.sum(value, axis=1, keepdims=True) * (1.0 / cells))
        tail = stacked(tail)
        factor = jnp.exp2(15.0 - level)
        for n in range(parts):
            grads[n, :body, :] = grads[n, :body, :] * factor
            grads[n, body:, :] = tail
        half = shares.shape[1] - TAIL
        level = exponent(jnp.max(top[...], axis=0, keepdims=True))
        factor = jnp.exp2(15.0 - level)
        for n in range(2):
            shares[n, :half, :] = shares[n, :half, :] * factor
            shares[n, half:, :] = stacked([level])


def coded(value):
    value = jnp.broadcast_to(value, (1, LANES))
    level = exponent(jnp.abs(value))
    left = value * jnp.exp2(-level)
    codes = [level]
    unit = 1024.0
    for _ in range(3):
        code = (left * unit + 12582912.0) - 12582912.0
        codes.append(code)
        left = left - code * (1.0 / unit)
        unit = unit * 1024.0
    return codes


def decoded(rows):
    level, first, second, third = [rows[n:n + 1, :] for n in range(4)]
    small = 1.0 / 1024.0
    return jnp.exp2(level) * (first + (second + third * small) * small) * small


def stacked(rows):
    place = lax.broadcasted_iota(jnp.int32, (TAIL, LANES), 0)
    out = jnp.zeros((TAIL, LANES), f32)
    for n, row in enumerate(rows):
        out = jnp.where(place == n, row, out)
    return out


def exponent(lanes):
    top = jnp.maximum(jnp.max(lanes, axis=1, keepdims=True), 1e-30)
    return jnp.broadcast_to(jnp.ceil(jnp.log(top) * (1.0 / math.log(2.0))), lanes.shape)


def join_kernel(mine, other, out):
    core = lax.axis_index("tm") % 2
    body = other.shape[0] - TAIL
    chips = out.shape[0]
    piece = body // chips
    own, far = mine[core, body:body + 1, :], other[body:body + 1, :]
    level = jnp.maximum(own, far) + 1.0
    own, far = jnp.exp2(own - level), jnp.exp2(far - level)
    for n in range(chips):
        rows = slice(n * piece, (n + 1) * piece)
        out[n, :piece, :] = mine[core, rows, :] * own + other[rows, :] * far
        out[n, piece:, :] = stacked([level])


def total_kernel(lift, mine, *refs):
    others, (out, factor) = refs[:-2], refs[-2:]
    piece = out.shape[0]
    here = lax.axis_index("tm") // 2
    levels = [mine[here, piece:piece + 1, :]] + [other[piece:piece + 1, :] for other in others]
    top = levels[0]
    for level in levels[1:]:
        top = jnp.maximum(top, level)
    top = top + lift
    total = mine[here, :piece, :] * jnp.exp2(levels[0] - top)
    for level, other in zip(levels[1:], others):
        total = total + other[:piece, :] * jnp.exp2(level - top)
    out[...] = total
    factor[...] = jnp.exp2(top - 15.0)


def gather_kernel(draws, tiles, parts, running, products, mine, *refs):
    others, (gathered, summary) = refs[:-2], refs[-2:]
    factors = running.shape[0]
    body = draws * tiles * factors
    here = lax.axis_index("series")
    tails = [mine[here, body:, :]] + [other[body:, :] for other in others]
    scales = [jnp.exp2(rows[0:1, :] - 15.0) for rows in tails]
    same = eye(factors)
    summary[0:1, :] = products[0:1, :]
    for d in range(draws):
        known = [decoded(rows[1 + 4 * d:5 + 4 * d, :]) for rows in tails]
        density = jnp.zeros((1, LANES), f32)
        for place in range(parts):
            for n in range(parts):
                density = density + jnp.where((here ^ n) == place, known[n], 0.0)
        summary[draws + 1 + d:draws + 2 + d, :] = density[:, :factors]
        leaving = jnp.zeros((factors, LANES), f32)
        for j in range(tiles):
            rows = slice((d * tiles + j) * factors, (d * tiles + j + 1) * factors)
            value = mine[here, rows, :] * scales[0]
            for other, scale in zip(others, scales[1:]):
                value = value + other[rows, :] * scale
            gathered[rows, :] = value
            leaving = leaving + value * running[:, j * LANES:(j + 1) * LANES]
        summary[d + 1:d + 2, :] = to_row(jnp.sum(leaving, axis=1, keepdims=True), same)


def unwind_kernel(tiles, decay, scale, gates, inner, weight, fade):
    factors = decay.shape[0]
    lane = lax.broadcasted_iota(jnp.int32, (factors, LANES), 1)
    sized = to_column(scale[...], eye(factors))
    beyond = jnp.ones((factors, 1), f32)
    for j in range(tiles - 1, -1, -1):
        part = slice(j * LANES, (j + 1) * LANES)
        a = decay[:, part]
        w = jnp.sqrt((1.0 - a) * (1.0 + a)) * sized
        weight[:, part] = w
        if j + 1 < tiles:
            after = decay[:, (j + 1) * LANES:(j + 2) * LANES][:, 0:1]
        else:
            after = jnp.ones((factors, 1), f32)
        run = jnp.where(lane < LANES - 1, pltpu.roll(a, LANES - 1, 1), after)
        for level in range(gates.shape[0]):
            step = 1 << level
            inside = lane < LANES - step
            gates[level, :, part] = jnp.where(inside, run, 0.0)
            run = run * jnp.where(inside, pltpu.roll(run, LANES - step, 1), 1.0)
        inner[:, part] = run
        fade[:, part] = w * run * beyond
        beyond = beyond * run[:, 0:1]


def backward_kernel(draws, tiles, gates, inner, grads, local):
    factors = inner.shape[0]
    carry = None
    for j in range(tiles - 1, -1, -1):
        part = slice(j * LANES, (j + 1) * LANES)
        rows = lambda d: slice((d * tiles + j) * factors, (d * tiles + j + 1) * factors)
        values = [grads[rows(d), :] for d in range(draws)]
        for level in range(gates.shape[0]):
            gate = gates[level, :, part]
            values = [p + gate * pltpu.roll(p, LANES - (1 << level), 1) for p in values]
        if carry is not None:
            values = [values[d] + inner[:, part] * carry[d] for d in range(draws)]
        for d in range(draws):
            local[d, :, part] = values[d]
        carry = [p[:, 0:1] for p in values]


def leave_kernel(draws, tiles, cells, count, *refs):
    pieces, refs = refs[:count], refs[count:]
    (local, fade, weight, innov), climb, (near, told, far, out, density, sems) = refs[:4], refs[4:-6], refs[-6:]
    lines, chips = pieces[0].shape[0], count // 2
    mine = lax.axis_index("tm")
    moves = []
    for n, piece in enumerate(pieces):
        side = (mine + n // chips) % 2
        start = pl.multiple_of((side * chips + ((mine // 2) ^ (n % chips))) * lines, lines)
        moves.append(pltpu.make_async_copy(piece, far.at[pl.ds(start, lines), :], sems.at[n]))
    for move in moves:
        move.start()
    factors = fade.shape[0]
    same = eye(factors)
    arriving, summed = entered(draws + 1, True, climb[0], climb[1:])
    columns = [to_column(arriving[d:d + 1, :], same) for d in range(draws)]
    for d in range(draws):
        density[d] = jnp.max(summed[d:d + 1, :]) * (1.0 / cells)
    moves.append(pltpu.make_async_copy(density, told, sems.at[count + 1]))
    moves[-1].start()
    for j in range(tiles):
        part = slice(j * LANES, (j + 1) * LANES)
        for d in range(draws):
            rows = pl.ds(j * draws + d, factors, stride=tiles * draws)
            out[rows, :] = weight[:, part] * local[d, :, part] + fade[:, part] * columns[d] - innov[rows, :]
    moves.append(pltpu.make_async_copy(out, near, sems.at[count]))
    moves[-1].start()
    for move in moves:
        move.wait()


def room(mebibytes):
    return pltpu.CompilerParams(vmem_limit_bytes=mebibytes << 20)


def shape(dims, kind):
    return jax.ShapeDtypeStruct(dims, kind)


def carried(summary, rows, backward):
    pairs = lax.axis_size("tm") // 2
    other = swap(summary, "tm", 1)
    whole = pl.pallas_call(
        functools.partial(pair_kernel, rows, backward, 1), out_shape=shape(summary.shape, f32), compiler_params=room(1)
    )(summary, other)
    return [other, whole] + [swap(whole, "tm", 2 * key) for key in range(1, pairs)]


def local(returns, innovations, decay_rate, innov_scale, loadings, noise_scale):
    factors, draws, steps = innovations.shape
    series = returns.shape[1]
    parts, spans = lax.axis_size("series"), lax.axis_size("tm")
    where, when = lax.axis_index("series"), lax.axis_index("tm")
    tiles = steps // LANES
    all_factors = factors * parts
    wide = all_factors * draws // LANES

    innov = innovations.reshape(factors, draws, tiles, LANES).transpose(0, 2, 1, 3)
    innov = innov.reshape(factors * tiles * draws, LANES)
    numbers = [where ^ key for key in range(parts)] + [1 - when % 2]
    numbers += [(when // 2) ^ key for key in range(spans // 2)]
    decay_rate, numbers = lax.optimization_barrier((decay_rate, numbers))
    seats, far_core = numbers[:parts], numbers[parts]
    chips_at = numbers[parts + 1:]
    spread, beyond, product, decays = pl.pallas_call(
        functools.partial(beyond_kernel, tiles),
        out_shape=(
            shape((factors, steps), f32),
            shape((factors, steps), f32),
            shape((1, factors), f32),
            shape((factors, steps), f32),
        ),
        name="beyond",
        cost_estimate=pl.CostEstimate(flops=2_000_000_000, bytes_accessed=1 << 20, transcendentals=0),
        compiler_params=room(2),
    )(decay_rate)
    pushes, summary, squares = pl.pallas_call(
        functools.partial(edge_kernel, draws, tiles),
        out_shape=(
            shape((draws, factors, steps), f32),
            shape((draws + 1, factors), f32),
            shape((draws, LANES), f32),
        ),
        name="edge",
        compiler_params=room(3),
    )(innov, innov_scale.reshape(1, factors), spread, beyond, product)
    local_paths, running = pl.pallas_call(
        functools.partial(forward_kernel, draws, tiles),
        out_shape=(shape((draws, factors, steps), f32), shape((factors, steps), f32)),
        name="forward_scan",
        compiler_params=room(4),
    )(decays, pushes)
    path_low = pl.pallas_call(
        functools.partial(enter_kernel, draws),
        out_shape=shape((draws, factors, steps), bf16),
        name="enter",
        compiler_params=room(2),
    )(local_paths, running, *carried(summary, draws + 1, False))

    pieces = [path_low] + [swap(path_low, "series", key) for key in range(1, parts)]
    noise = noise_scale.reshape(series // LANES, LANES)
    loads = loadings.transpose(1, 0, 2)
    loads_t = loadings.transpose(1, 2, 0)
    rows = min(1024, series)
    body = draws * tiles * factors
    still = lambda dims: pl.BlockSpec(dims, lambda i: (0,) * len(dims))
    size = series * wide
    half, piece = size // 2, size // spans
    grads, load_share = pl.pallas_call(
        functools.partial(residual_kernel, draws, parts, series // rows),
        out_shape=(
            shape((parts, body + TAIL, LANES), f32),
            shape((2, half + TAIL, LANES), f32),
        ),
        grid_spec=pl.GridSpec(
            grid=() if rows == series else (series // rows,),
            in_specs=[pl.BlockSpec(memory_space=pltpu.VMEM)] * (parts + 5) if rows == series else [still((draws, factors, steps))] * parts
            + [
                pl.BlockSpec((steps, rows), lambda i: (0, i)),
                pl.BlockSpec((draws, rows, all_factors), lambda i: (0, i, 0)),
                pl.BlockSpec((draws, all_factors, rows), lambda i: (0, 0, i)),
                still((series // LANES, LANES)),
                still((draws, LANES)),
            ],
            out_specs=[pl.BlockSpec(memory_space=pltpu.VMEM)] * 2 if rows == series else [
                still((parts, body + TAIL, LANES)),
                still((2, half + TAIL, LANES)),
            ],
            scratch_shapes=[
                pltpu.VMEM((draws, all_factors, steps), bf16),
                pltpu.VMEM((draws, LANES), f32),
                pltpu.VMEM((8, LANES), f32),
            ],
        ),
        name="residual",
        compiler_params=room(28),
    )(*pieces, returns, loads, loads_t, noise, squares)

    pick = lambda value, place: lax.dynamic_slice(value, (place, 0, 0), (1,) + value.shape[1:], allow_negative_indices=False)[0]
    sent = [pick(grads, place).astype(f16) for place in seats[1:]]
    arrived = [swap(value, "series", key) for key, value in enumerate(sent, 1)]

    chips = spans // 2
    whole = pl.BlockSpec(memory_space=pltpu.VMEM)
    distant = pl.BlockSpec(memory_space=pltpu.HBM)
    other = swap(pick(load_share, far_core).astype(f16), "tm", 1).astype(f32)
    kept = pl.pallas_call(
        join_kernel,
        out_shape=shape((chips, piece + TAIL, LANES), f32),
        in_specs=[whole, whole],
        out_specs=whole,
        name="join",
        compiler_params=room(8),
    )(load_share, other)
    others = [swap(pick(kept, chips_at[key]).astype(f16), "tm", 2 * key).astype(f32) for key in range(1, chips)]
    total, factor = pl.pallas_call(
        functools.partial(total_kernel, float(math.ceil(math.log2(chips)))),
        out_shape=(shape((piece, LANES), f32), shape((1, LANES), f32)),
        in_specs=[whole] * chips,
        out_specs=(whole, whole),
        name="total",
        compiler_params=room(4),
    )(kept, *others)
    total = lax.optimization_barrier(total.astype(f16))
    totals = [total] + [swap(total, "tm", 2 * key) for key in range(1, chips)]
    passed = [swap(value, "tm", 1) for value in totals]
    path_grads, leaving = pl.pallas_call(
        functools.partial(gather_kernel, draws, tiles, parts),
        out_shape=(shape((body, LANES), f32), shape((2 * draws + 1, factors), f32)),
        name="gather",
        compiler_params=room(4),
    )(running, summary, grads, *[value.astype(f32) for value in arrived])
    levels = LANES.bit_length() - 1
    flat = shape((factors, steps), f32)
    gates, inner, weight, fade = pl.pallas_call(
        functools.partial(unwind_kernel, tiles),
        out_shape=(shape((levels, factors, steps), f32), flat, flat, flat),
        name="unwind",
        compiler_params=room(4),
    )(decays, innov_scale.reshape(1, factors))
    local_adjoint = pl.pallas_call(
        functools.partial(backward_kernel, draws, tiles),
        out_shape=shape((draws, factors, steps), f32),
        name="backward_scan",
        compiler_params=room(4),
    )(gates, inner, path_grads)
    climb = carried(leaving, draws + 1, True)
    grad_innov, log_density, grad_load = pl.pallas_call(
        functools.partial(leave_kernel, draws, tiles, float(spans * parts), 2 * chips),
        out_shape=(shape(innov.shape, f32), shape((draws,), f32), shape((size, LANES), f32)),
        in_specs=[whole] * (2 * chips + 4 + len(climb)),
        out_specs=(distant, distant, distant),
        scratch_shapes=[pltpu.VMEM(innov.shape, f32), pltpu.SMEM((draws,), f32), pltpu.SemaphoreType.DMA((2 * chips + 2,))],
        name="leave",
        compiler_params=room(6),
    )(*[value.astype(f32) * factor for value in totals + passed], local_adjoint, fade, weight, innov, *climb)
    grad_load = grad_load.reshape(series, all_factors // LANES, draws, LANES).transpose(0, 2, 1, 3)
    grad_load = grad_load.reshape(series, draws, all_factors)
    grad_innov = grad_innov.reshape(factors, tiles, draws, LANES).transpose(0, 2, 1, 3)
    grad_innov = grad_innov.reshape(factors, draws, steps)

    return (grad_innov, grad_load, log_density)


def solution(mesh):
    placed = (
        P("tm", "series"),
        P("series", None, "tm"),
        P("series", "tm"),
        P("series"),
        P("series", None, None),
        P("series"),
    )

    return jax.shard_map(
        local,
        mesh=mesh,
        in_specs=placed,
        out_specs=(P("series", None, "tm"), P("series", None, None), P()),
        check_vma=False,
    )
```

```python
import functools
import math

import jax
import jax.numpy as jnp
from jax import lax
from jax.experimental import pallas as pl
from jax.experimental.pallas import tpu as pltpu
from jax.sharding import PartitionSpec as P


freedom = 5.0
LANES = 128
TAIL = 16
f32 = jnp.float32
bf16 = jnp.bfloat16
f16 = jnp.float16


def swap(value, axis, key):
    count = lax.axis_size(axis)
    return lax.ppermute(value, axis, [(i, i ^ key) for i in range(count)])


def eye(size):
    rows = lax.broadcasted_iota(jnp.int32, (size, size), 0)
    return rows == lax.broadcasted_iota(jnp.int32, (size, size), 1)


def to_column(row, same):
    return jnp.sum(jnp.where(same, row, 0.0), axis=1, keepdims=True)


def to_row(column, same):
    return jnp.sum(jnp.where(same, column, 0.0), axis=0, keepdims=True)


def tile_scan(decay, pushes, backward):
    lane = lax.broadcasted_iota(jnp.int32, decay.shape, 1)
    width = decay.shape[1]
    step = 1
    while step < width:
        turn = width - step if backward else step
        inside = lane < width - step if backward else lane >= step
        gate = jnp.where(inside, decay, 0.0)
        pushes = [p + gate * pltpu.roll(p, turn, 1) for p in pushes]
        decay = decay * jnp.where(inside, pltpu.roll(decay, turn, 1), 1.0)
        step *= 2
    return decay, pushes


def block_scan(decays, pushes, backward):
    tiles = len(decays)
    draws = len(pushes[0])
    order = range(tiles - 1, -1, -1) if backward else range(tiles)
    edge = slice(0, 1) if backward else slice(LANES - 1, LANES)
    run, out = [None] * tiles, [None] * tiles
    carry = None
    for j in order:
        a, b = tile_scan(decays[j], pushes[j], backward)
        if carry is not None:
            b = [b[d] + a * carry[1][d] for d in range(draws)]
            a = a * carry[0]
        run[j], out[j] = a, b
        carry = (a[:, edge], [x[:, edge] for x in b])
    return run, out, carry


def beyond_kernel(tiles, decay, spread, beyond, product, held):
    factors = decay.shape[0]
    held[...] = decay[...]
    lane = lax.broadcasted_iota(jnp.int32, (factors, LANES), 1)
    after = jnp.ones((factors, 1), f32)
    for j in range(tiles - 1, -1, -1):
        part = slice(j * LANES, (j + 1) * LANES)
        a = decay[:, part]
        spread[:, part] = jnp.sqrt((1.0 - a) * (1.0 + a))
        run, _ = tile_scan(a, [], True)
        beyond[:, part] = jnp.where(lane < LANES - 1, pltpu.roll(run, LANES - 1, 1), 1.0) * after
        after = after * run[:, 0:1]
    product[...] = to_row(after, eye(factors))


def edge_kernel(draws, tiles, innov, scale, spread, beyond, product, pushes, summary, squares):
    factors = spread.shape[0]
    same = eye(factors)
    column = to_column(scale[...], same)
    total = [jnp.zeros((factors, LANES), f32)] * draws
    ends = [jnp.zeros((factors, LANES), f32)] * draws
    for j in range(tiles):
        part = slice(j * LANES, (j + 1) * LANES)
        w = spread[:, part] * column
        for d in range(draws):
            x = innov[pl.ds(j * draws + d, factors, stride=tiles * draws), :]
            push = w * x
            pushes[d, :, part] = push
            total[d] = total[d] + x * x
            ends[d] = ends[d] + push * beyond[:, part]
    summary[0:1, :] = product[...]
    for d in range(draws):
        summary[d + 1:d + 2, :] = to_row(jnp.sum(ends[d], axis=1, keepdims=True), same)
        squares[d:d + 1, :] = jnp.sum(total[d], axis=0, keepdims=True)


def forward_kernel(draws, tiles, decay, pushed, local, running):
    parts = [slice(j * LANES, (j + 1) * LANES) for j in range(tiles)]
    decays = [decay[:, part] for part in parts]
    pushes = [[pushed[d, :, part] for d in range(draws)] for part in parts]
    run, out, _ = block_scan(decays, pushes, False)
    for j in range(tiles):
        running[:, j * LANES:(j + 1) * LANES] = run[j]
        for d in range(draws):
            local[d, :, j * LANES:(j + 1) * LANES] = out[j][d]


def seat(backward):
    count, mine = lax.axis_size("tm"), lax.axis_index("tm")
    return count - 1 - mine if backward else mine


def pair_kernel(rows, backward, bit, summary, other, whole):
    later = (seat(backward) // bit) % 2 == 1
    mine, theirs = summary[...], other[...]
    first, second = jnp.where(later, theirs, mine), jnp.where(later, mine, theirs)
    whole[0:1, :] = first[0:1] * second[0:1]
    whole[1:rows, :] = second[0:1] * first[1:rows] + second[1:rows]
    if rows < mine.shape[0]:
        whole[rows:, :] = first[rows:] + second[rows:]


def entered(rows, backward, other, totals):
    mine = seat(backward)
    later, pair, pairs = mine % 2 == 1, mine // 2, len(totals)
    theirs = other[...]
    values = [total[...] for total in totals]
    entering = jnp.zeros_like(theirs[1:rows])
    summed = jnp.zeros_like(theirs[rows:]) if rows < theirs.shape[0] else None
    for place in range(pairs):
        here = values[0]
        for key in range(1, pairs):
            here = jnp.where((pair ^ key) == place, values[key], here)
        entering = jnp.where(place < pair, here[0:1] * entering + here[1:rows], entering)
        if summed is not None:
            summed = summed + here[rows:]
    return jnp.where(later, theirs[0:1] * entering + theirs[1:rows], entering), summed


def enter_kernel(draws, local, running, other, *refs):
    totals, path = refs[:-1], refs[-1]
    same = eye(running.shape[0])
    entering, _ = entered(draws + 1, False, other, totals)
    for d in range(draws):
        column = to_column(entering[d:d + 1, :], same)
        path[d] = (local[d] + running[...] * column).astype(bf16)


def when(condition):
    return (lambda body: body()) if condition is True else pl.when(condition)


def residual_kernel(draws, parts, count, *refs):
    pieces, (returns, loads, loads_t, noise, squares, grads, shares, paths, density, top) = refs[:parts], refs[parts:]
    factors = pieces[0].shape[1]
    step = 0 if count == 1 else pl.program_id(0)
    wide = paths.shape[1] // LANES
    share_rows = returns.shape[1] // 2 if count == 1 else returns.shape[1]
    side = step // max(count // 2, 1)
    base = (step % max(count // 2, 1)) * (share_rows * wide * draws)

    @when(step == 0)
    def _():
        for n in range(parts):
            start = pl.multiple_of((lax.axis_index("series") ^ n) * factors, factors)
            paths[:, pl.ds(start, factors), :] = pieces[n][...]
        if count > 1:
            grads[...] = jnp.zeros_like(grads)
        density[...] = jnp.zeros_like(density)
        top[...] = jnp.zeros_like(top)

    seen = returns[...].T.astype(f32)
    rows = seen.shape[0]
    same = eye(LANES)
    groups = rows // LANES
    spread = [to_column(noise[pl.ds(step * groups + g, 1), :], same) for g in range(groups)]
    spread = jnp.concatenate(spread, axis=0)
    s2 = freedom * (spread * spread)
    inverse = 1.0 / s2
    tiles = seen.shape[1] // LANES
    half = rows // 2
    for d in range(draws):
        fitted = jnp.dot(loads[d], paths[d], preferred_element_type=f32)
        residual = seen - fitted
        square = residual * residual
        pulled = ((freedom + 1.0) * residual / (s2 + square)).astype(bf16)
        ratio = square * inverse
        first, second = ratio[:half], ratio[half:]
        both = jnp.log1p(first + second * (1.0 + first))
        both = jnp.sum(both, axis=0, keepdims=True)
        lanes = both[:, :LANES]
        for j in range(1, both.shape[1] // LANES):
            lanes = lanes + both[:, j * LANES:(j + 1) * LANES]
        density[d:d + 1, :] += lanes
        product = jnp.dot(loads_t[d], pulled, preferred_element_type=f32)
        for n in range(parts):
            for j in range(tiles):
                to = slice((d * tiles + j) * factors, (d * tiles + j + 1) * factors)
                part = product[n * factors:(n + 1) * factors, j * LANES:(j + 1) * LANES]
                grads[n, to, :] = part if count == 1 else grads[n, to, :] + part
        share = lax.dot_general(pulled, paths[d], (((1,), (1,)), ((), ())), preferred_element_type=f32)
        most = top[...]
        for j in range(wide):
            tile = share[:, j * LANES:(j + 1) * LANES]
            for part in range(rows // share_rows):
                piece = tile[part * share_rows:(part + 1) * share_rows]
                shares[side + part, pl.ds(base + (j * draws + d), share_rows, stride=wide * draws), :] = piece
            most = jnp.maximum(most, jnp.max(jnp.abs(tile).reshape(rows // 8, 8, LANES), axis=0))
        top[...] = most

    @when(step == count - 1)
    def _():
        body = draws * tiles * factors
        cells = count * rows * seen.shape[1]
        peak = jnp.zeros((1, LANES), f32)
        for n in range(parts):
            peak = jnp.maximum(peak, jnp.max(jnp.abs(grads[n, :body, :]), axis=0, keepdims=True))
        level = exponent(peak)
        tail = [level]
        for d in range(draws):
            value = -(freedom + 1.0) * 0.5 * density[d:d + 1, :] - 0.5 * squares[d:d + 1, :]
            tail += coded(jnp.sum(value, axis=1, keepdims=True) * (1.0 / cells))
        tail = stacked(tail)
        factor = jnp.exp2(15.0 - level)
        for n in range(parts):
            grads[n, :body, :] = grads[n, :body, :] * factor
            grads[n, body:, :] = tail
        half = shares.shape[1] - TAIL
        level = exponent(jnp.max(top[...], axis=0, keepdims=True))
        factor = jnp.exp2(15.0 - level)
        for n in range(2):
            shares[n, :half, :] = shares[n, :half, :] * factor
            shares[n, half:, :] = stacked([level])


def coded(value):
    value = jnp.broadcast_to(value, (1, LANES))
    level = exponent(jnp.abs(value))
    left = value * jnp.exp2(-level)
    codes = [level]
    unit = 1024.0
    for _ in range(3):
        code = (left * unit + 12582912.0) - 12582912.0
        codes.append(code)
        left = left - code * (1.0 / unit)
        unit = unit * 1024.0
    return codes


def decoded(rows):
    level, first, second, third = [rows[n:n + 1, :] for n in range(4)]
    small = 1.0 / 1024.0
    return jnp.exp2(level) * (first + (second + third * small) * small) * small


def stacked(rows):
    place = lax.broadcasted_iota(jnp.int32, (TAIL, LANES), 0)
    out = jnp.zeros((TAIL, LANES), f32)
    for n, row in enumerate(rows):
        out = jnp.where(place == n, row, out)
    return out


def exponent(lanes):
    top = jnp.maximum(jnp.max(lanes, axis=1, keepdims=True), 1e-30)
    return jnp.broadcast_to(jnp.ceil(jnp.log(top) * (1.0 / math.log(2.0))), lanes.shape)


def join_kernel(mine, other, out):
    core = lax.axis_index("tm") % 2
    body = other.shape[0] - TAIL
    chips = out.shape[0]
    piece = body // chips
    own, far = mine[core, body:body + 1, :], other[body:body + 1, :]
    level = jnp.maximum(own, far) + 1.0
    own, far = jnp.exp2(own - level), jnp.exp2(far - level)
    for n in range(chips):
        rows = slice(n * piece, (n + 1) * piece)
        out[n, :piece, :] = mine[core, rows, :] * own + other[rows, :] * far
        out[n, piece:, :] = stacked([level])


def total_kernel(lift, mine, *refs):
    others, (out, factor) = refs[:-2], refs[-2:]
    piece = out.shape[0]
    here = lax.axis_index("tm") // 2
    levels = [mine[here, piece:piece + 1, :]] + [other[piece:piece + 1, :] for other in others]
    top = levels[0]
    for level in levels[1:]:
        top = jnp.maximum(top, level)
    top = top + lift
    total = mine[here, :piece, :] * jnp.exp2(levels[0] - top)
    for level, other in zip(levels[1:], others):
        total = total + other[:piece, :] * jnp.exp2(level - top)
    out[...] = total
    factor[...] = jnp.exp2(top - 15.0)


def gather_kernel(draws, tiles, parts, running, products, mine, *refs):
    others, (gathered, summary) = refs[:-2], refs[-2:]
    factors = running.shape[0]
    body = draws * tiles * factors
    here = lax.axis_index("series")
    tails = [mine[here, body:, :]] + [other[body:, :] for other in others]
    scales = [jnp.exp2(rows[0:1, :] - 15.0) for rows in tails]
    same = eye(factors)
    summary[0:1, :] = products[0:1, :]
    for d in range(draws):
        known = [decoded(rows[1 + 4 * d:5 + 4 * d, :]) for rows in tails]
        density = jnp.zeros((1, LANES), f32)
        for place in range(parts):
            for n in range(parts):
                density = density + jnp.where((here ^ n) == place, known[n], 0.0)
        summary[draws + 1 + d:draws + 2 + d, :] = density[:, :factors]
        leaving = jnp.zeros((factors, LANES), f32)
        for j in range(tiles):
            rows = slice((d * tiles + j) * factors, (d * tiles + j + 1) * factors)
            value = mine[here, rows, :] * scales[0]
            for other, scale in zip(others, scales[1:]):
                value = value + other[rows, :] * scale
            gathered[rows, :] = value
            leaving = leaving + value * running[:, j * LANES:(j + 1) * LANES]
        summary[d + 1:d + 2, :] = to_row(jnp.sum(leaving, axis=1, keepdims=True), same)


def unwind_kernel(tiles, decay, scale, gates, inner, weight, fade):
    factors = decay.shape[0]
    lane = lax.broadcasted_iota(jnp.int32, (factors, LANES), 1)
    sized = to_column(scale[...], eye(factors))
    beyond = jnp.ones((factors, 1), f32)
    for j in range(tiles - 1, -1, -1):
        part = slice(j * LANES, (j + 1) * LANES)
        a = decay[:, part]
        w = jnp.sqrt((1.0 - a) * (1.0 + a)) * sized
        weight[:, part] = w
        if j + 1 < tiles:
            after = decay[:, (j + 1) * LANES:(j + 2) * LANES][:, 0:1]
        else:
            after = jnp.ones((factors, 1), f32)
        run = jnp.where(lane < LANES - 1, pltpu.roll(a, LANES - 1, 1), after)
        for level in range(gates.shape[0]):
            step = 1 << level
            inside = lane < LANES - step
            gates[level, :, part] = jnp.where(inside, run, 0.0)
            run = run * jnp.where(inside, pltpu.roll(run, LANES - step, 1), 1.0)
        inner[:, part] = run
        fade[:, part] = w * run * beyond
        beyond = beyond * run[:, 0:1]


def backward_kernel(draws, tiles, gates, inner, grads, local):
    factors = inner.shape[0]
    carry = None
    for j in range(tiles - 1, -1, -1):
        part = slice(j * LANES, (j + 1) * LANES)
        rows = lambda d: slice((d * tiles + j) * factors, (d * tiles + j + 1) * factors)
        values = [grads[rows(d), :] for d in range(draws)]
        for level in range(gates.shape[0]):
            gate = gates[level, :, part]
            values = [p + gate * pltpu.roll(p, LANES - (1 << level), 1) for p in values]
        if carry is not None:
            values = [values[d] + inner[:, part] * carry[d] for d in range(draws)]
        for d in range(draws):
            local[d, :, part] = values[d]
        carry = [p[:, 0:1] for p in values]


def leave_kernel(draws, tiles, cells, count, *refs):
    pieces, refs = refs[:count], refs[count:]
    (local, fade, weight, innov), climb, (near, told, far, out, density, sems) = refs[:4], refs[4:-6], refs[-6:]
    lines, chips = pieces[0].shape[0], count // 2
    mine = lax.axis_index("tm")
    moves = []
    for n, piece in enumerate(pieces):
        side = (mine + n // chips) % 2
        start = pl.multiple_of((side * chips + ((mine // 2) ^ (n % chips))) * lines, lines)
        moves.append(pltpu.make_async_copy(piece, far.at[pl.ds(start, lines), :], sems.at[n]))
    for move in moves:
        move.start()
    factors = fade.shape[0]
    same = eye(factors)
    arriving, summed = entered(draws + 1, True, climb[0], climb[1:])
    columns = [to_column(arriving[d:d + 1, :], same) for d in range(draws)]
    for d in range(draws):
        density[d] = jnp.max(summed[d:d + 1, :]) * (1.0 / cells)
    moves.append(pltpu.make_async_copy(density, told, sems.at[count + 1]))
    moves[-1].start()
    share = factors // 2
    deep = share * tiles * draws
    for side in range(2):
        some = slice(side * share, (side + 1) * share)
        for j in range(tiles):
            part = slice(j * LANES, (j + 1) * LANES)
            for d in range(draws):
                rows = pl.ds(side * deep + j * draws + d, share, stride=tiles * draws)
                value = weight[some, part] * local[d, some, part] + fade[some, part] * columns[d][some]
                out[rows, :] = value - innov[rows, :]
        block = pl.ds(side * deep, deep)
        moves.append(pltpu.make_async_copy(out.at[block, :], near.at[block, :], sems.at[count + 2 * side]))
        moves[-1].start()
    for move in moves:
        move.wait()


def room(mebibytes):
    return pltpu.CompilerParams(vmem_limit_bytes=mebibytes << 20)


def shape(dims, kind):
    return jax.ShapeDtypeStruct(dims, kind)


def carried(summary, rows, backward):
    pairs = lax.axis_size("tm") // 2
    other = swap(summary, "tm", 1)
    whole = pl.pallas_call(
        functools.partial(pair_kernel, rows, backward, 1), out_shape=shape(summary.shape, f32), compiler_params=room(1)
    )(summary, other)
    return [other, whole] + [swap(whole, "tm", 2 * key) for key in range(1, pairs)]


def local(returns, innovations, decay_rate, innov_scale, loadings, noise_scale):
    factors, draws, steps = innovations.shape
    series = returns.shape[1]
    parts, spans = lax.axis_size("series"), lax.axis_size("tm")
    where, when = lax.axis_index("series"), lax.axis_index("tm")
    tiles = steps // LANES
    all_factors = factors * parts
    wide = all_factors * draws // LANES

    innov = innovations.reshape(factors, draws, tiles, LANES).transpose(0, 2, 1, 3)
    innov = innov.reshape(factors * tiles * draws, LANES)
    numbers = [where ^ key for key in range(parts)] + [1 - when % 2]
    numbers += [(when // 2) ^ key for key in range(spans // 2)]
    decay_rate, numbers = lax.optimization_barrier((decay_rate, numbers))
    seats, far_core = numbers[:parts], numbers[parts]
    chips_at = numbers[parts + 1:]
    spread, beyond, product, decays = pl.pallas_call(
        functools.partial(beyond_kernel, tiles),
        out_shape=(
            shape((factors, steps), f32),
            shape((factors, steps), f32),
            shape((1, factors), f32),
            shape((factors, steps), f32),
        ),
        name="beyond",
        cost_estimate=pl.CostEstimate(flops=2_000_000_000, bytes_accessed=1 << 20, transcendentals=0),
        compiler_params=room(2),
    )(decay_rate)
    pushes, summary, squares = pl.pallas_call(
        functools.partial(edge_kernel, draws, tiles),
        out_shape=(
            shape((draws, factors, steps), f32),
            shape((draws + 1, factors), f32),
            shape((draws, LANES), f32),
        ),
        name="edge",
        compiler_params=room(3),
    )(innov, innov_scale.reshape(1, factors), spread, beyond, product)
    local_paths, running = pl.pallas_call(
        functools.partial(forward_kernel, draws, tiles),
        out_shape=(shape((draws, factors, steps), f32), shape((factors, steps), f32)),
        name="forward_scan",
        compiler_params=room(4),
    )(decays, pushes)
    path_low = pl.pallas_call(
        functools.partial(enter_kernel, draws),
        out_shape=shape((draws, factors, steps), bf16),
        name="enter",
        compiler_params=room(2),
    )(local_paths, running, *carried(summary, draws + 1, False))

    pieces = [path_low] + [swap(path_low, "series", key) for key in range(1, parts)]
    noise = noise_scale.reshape(series // LANES, LANES)
    loads = loadings.transpose(1, 0, 2)
    loads_t = loadings.transpose(1, 2, 0)
    rows = min(1024, series)
    body = draws * tiles * factors
    still = lambda dims: pl.BlockSpec(dims, lambda i: (0,) * len(dims))
    size = series * wide
    half, piece = size // 2, size // spans
    grads, load_share = pl.pallas_call(
        functools.partial(residual_kernel, draws, parts, series // rows),
        out_shape=(
            shape((parts, body + TAIL, LANES), f32),
            shape((2, half + TAIL, LANES), f32),
        ),
        grid_spec=pl.GridSpec(
            grid=() if rows == series else (series // rows,),
            in_specs=[pl.BlockSpec(memory_space=pltpu.VMEM)] * (parts + 5) if rows == series else [still((draws, factors, steps))] * parts
            + [
                pl.BlockSpec((steps, rows), lambda i: (0, i)),
                pl.BlockSpec((draws, rows, all_factors), lambda i: (0, i, 0)),
                pl.BlockSpec((draws, all_factors, rows), lambda i: (0, 0, i)),
                still((series // LANES, LANES)),
                still((draws, LANES)),
            ],
            out_specs=[pl.BlockSpec(memory_space=pltpu.VMEM)] * 2 if rows == series else [
                still((parts, body + TAIL, LANES)),
                still((2, half + TAIL, LANES)),
            ],
            scratch_shapes=[
                pltpu.VMEM((draws, all_factors, steps), bf16),
                pltpu.VMEM((draws, LANES), f32),
                pltpu.VMEM((8, LANES), f32),
            ],
        ),
        name="residual",
        compiler_params=room(28),
    )(*pieces, returns, loads, loads_t, noise, squares)

    pick = lambda value, place: lax.dynamic_slice(value, (place, 0, 0), (1,) + value.shape[1:], allow_negative_indices=False)[0]
    sent = [pick(grads, place).astype(f16) for place in seats[1:]]
    arrived = [swap(value, "series", key) for key, value in enumerate(sent, 1)]

    chips = spans // 2
    whole = pl.BlockSpec(memory_space=pltpu.VMEM)
    distant = pl.BlockSpec(memory_space=pltpu.HBM)
    other = swap(pick(load_share, far_core).astype(f16), "tm", 1).astype(f32)
    kept = pl.pallas_call(
        join_kernel,
        out_shape=shape((chips, piece + TAIL, LANES), f32),
        in_specs=[whole, whole],
        out_specs=whole,
        name="join",
        compiler_params=room(8),
    )(load_share, other)
    others = [swap(pick(kept, chips_at[key]).astype(f16), "tm", 2 * key).astype(f32) for key in range(1, chips)]
    total, factor = pl.pallas_call(
        functools.partial(total_kernel, float(math.ceil(math.log2(chips)))),
        out_shape=(shape((piece, LANES), f32), shape((1, LANES), f32)),
        in_specs=[whole] * chips,
        out_specs=(whole, whole),
        name="total",
        compiler_params=room(4),
    )(kept, *others)
    total = lax.optimization_barrier(total.astype(f16))
    totals = [total] + [swap(total, "tm", 2 * key) for key in range(1, chips)]
    passed = [swap(value, "tm", 1) for value in totals]
    path_grads, leaving = pl.pallas_call(
        functools.partial(gather_kernel, draws, tiles, parts),
        out_shape=(shape((body, LANES), f32), shape((2 * draws + 1, factors), f32)),
        name="gather",
        compiler_params=room(4),
    )(running, summary, grads, *[value.astype(f32) for value in arrived])
    levels = LANES.bit_length() - 1
    flat = shape((factors, steps), f32)
    gates, inner, weight, fade = pl.pallas_call(
        functools.partial(unwind_kernel, tiles),
        out_shape=(shape((levels, factors, steps), f32), flat, flat, flat),
        name="unwind",
        compiler_params=room(4),
    )(decays, innov_scale.reshape(1, factors))
    local_adjoint = pl.pallas_call(
        functools.partial(backward_kernel, draws, tiles),
        out_shape=shape((draws, factors, steps), f32),
        name="backward_scan",
        compiler_params=room(4),
    )(gates, inner, path_grads)
    climb = carried(leaving, draws + 1, True)
    grad_innov, log_density, grad_load = pl.pallas_call(
        functools.partial(leave_kernel, draws, tiles, float(spans * parts), 2 * chips),
        out_shape=(shape(innov.shape, f32), shape((draws,), f32), shape((size, LANES), f32)),
        in_specs=[whole] * (2 * chips + 4 + len(climb)),
        out_specs=(distant, distant, distant),
        scratch_shapes=[pltpu.VMEM(innov.shape, f32), pltpu.SMEM((draws,), f32), pltpu.SemaphoreType.DMA((2 * chips + 3,))],
        name="leave",
        compiler_params=room(6),
    )(*[value.astype(f32) * factor for value in totals + passed], local_adjoint, fade, weight, innov, *climb)
    grad_load = grad_load.reshape(series, all_factors // LANES, draws, LANES).transpose(0, 2, 1, 3)
    grad_load = grad_load.reshape(series, draws, all_factors)
    grad_innov = grad_innov.reshape(factors, tiles, draws, LANES).transpose(0, 2, 1, 3)
    grad_innov = grad_innov.reshape(factors, draws, steps)

    return (grad_innov, grad_load, log_density)


def solution(mesh):
    placed = (
        P("tm", "series"),
        P("series", None, "tm"),
        P("series", "tm"),
        P("series"),
        P("series", None, None),
        P("series"),
    )

    return jax.shard_map(
        local,
        mesh=mesh,
        in_specs=placed,
        out_specs=(P("series", None, "tm"), P("series", None, None), P()),
        check_vma=False,
    )
```
